32 devices in a mesh: gx: 2 (over x), gy: 4 (over z), gz: 4 (over y, core).
Axes of the slice: x: 2, y: 2, z: 4, core: 2. Of those that a mesh axis runs over, the one named last changes fastest.
Arguments:
- perturb: float32 [27, 16, 64, 512], P(None, 'gx', 'gy', 'gz'), may hold values from -2.5 to 2.5
- density: float32 [16, 64, 512], P('gx', 'gy', 'gz'), may hold values from 0.9 to 1.1
- velocity: float32 [3, 16, 64, 512], P(None, 'gx', 'gy', 'gz'), may hold values from -0.12 to 0.12
- excitation: float32 [16, 64, 512], P('gx', 'gy', 'gz'), may hold values from 0.0001 to 0.2
- solid_flag: int32 [16, 64, 512], P('gx', 'gy', 'gz'), may hold values 0 or 1
- panel_cell: int32 [8192], P(('gx', 'gy', 'gz')), may hold values from 0 to 16383
- panel_owner: int32 [8192], P(('gx', 'gy', 'gz')), may hold values from 0 to 7, as said below
- panel_area: float32 [3, 8192], P(None, ('gx', 'gy', 'gz')), may hold values from -4 to 4
- weights: bfloat16 [4, 16384, 1024], P(None, ('gx', 'gy', 'gz')), may hold values from -1.796875 to 1.796875
- bin_offset: int32 [256, 8], P(('gx', 'gy', 'gz')), may hold values from 0 to 124
Outputs:
- final_density: float32 [16, 64, 512], P('gx', 'gy', 'gz')
- final_velocity: float32 [3, 16, 64, 512], P(None, 'gx', 'gy', 'gz')
- signal: float32 [1024, 128], P(('gx', 'gy', 'gz'))
The draws below stay inside these ranges and needn't reach their ends.
Inputs may be any that keep to these rules, and one draw needn't show every extreme that they name: `panel_owner`: the slots of a device name owners of its vertical layer; at most 64 slots of one device name the same owner, and in each vertical layer one owner is named by exactly 64 slots of every device of the layer.
All inputs are finite; a program needn't handle non-finite values. No bound on the sum of `solid_flag` on one device may be relied on, other than what follows from the above.
Results may differ from the reference program's by a relative error of at most 0.0029.
Values may be sent and summed in bfloat16 or wider, within the bound.
No kernel may reach another device: no remote copies, remote signals or barrier semaphores. Data moves between devices by JAX's collectives and lax.ppermute only.
A program may use at most 128 MiB of HBM per device.

```python
import math
import jax
import jax.numpy as jnp
import numpy as np
from jax import lax

BX = 8
BY = 16
BZ = 128
PS = 256
STEPS = 4
PTILE = 64
OTILE = 128
NOBS = 1024
NB = 128
NX = 16
NY = 64
NZ = 512
GROUP = 8
CAP = 64
ROWS = 512
SLOTS = 8192
ALLROWS = 16384
TILES = 256
N_GY = 4
N_GZ = 4
DEVICES = 32


def draw_panel_owner(key, part):
    hot_key, pool_key, order_key = jax.random.split(key, 3)
    device_count = SLOTS // PS
    layers = device_count // GROUP
    hot_owner = jax.random.randint(hot_key, (layers,), 0, GROUP)
    device_list = jnp.arange(device_count)
    hot_device = hot_owner[device_list % layers]
    base_pool = jnp.repeat(jnp.arange(GROUP - 1, dtype=jnp.int32), CAP)

    def one_device(pool_seed, order_seed, hot_one):
        mixed = jax.random.permutation(pool_seed, base_pool)[:PS - CAP]
        others = mixed + (mixed >= hot_one).astype(jnp.int32)
        whole_list = jnp.concatenate([jnp.zeros((CAP,), jnp.int32) + hot_one, others.astype(jnp.int32)])
        return jax.random.permutation(order_seed, whole_list)
    pool_keys = jax.random.split(pool_key, device_count)
    order_keys = jax.random.split(order_key, device_count)
    return jax.vmap(one_device)(pool_keys, order_keys, hot_device.astype(jnp.int32)).reshape(-1).astype(jnp.int32)


def plant(values, key, low, top_value):
    longest = values.shape.index(max(values.shape))
    spots = []
    for shift in (0, 1):
        where = [jax.random.randint(jax.random.fold_in(key, axis), (), 0, length) for axis, length in enumerate(values.shape)]
        where[longest] = (where[longest] + shift) % values.shape[longest]
        spots.append(tuple(where))
    return values.at[spots[0]].set(low).at[spots[1]].set(top_value)


def spiked(drawn, own_key, source, target, parts, factor):
    def block_of(dim):
        return (jnp.arange(drawn.shape[dim]) // (drawn.shape[dim] // parts)).reshape((-1,) + (1,) * (drawn.ndim - 1 - dim))

    first = jax.random.permutation(own_key, parts)[block_of(target)]
    far = (block_of(target) + parts // 2) % parts
    return jnp.where((block_of(source) == first) | (block_of(source) == far), factor * drawn, drawn)


def block_scale(own_key, extent, cuts, smallest, high):
    def one(position, shards_of):
        heights = jax.random.uniform(jax.random.fold_in(jax.random.fold_in(own_key, 6), position), (shards_of,), jnp.float32, smallest / len(cuts), high / len(cuts))
        return jnp.repeat(jnp.exp(heights), extent[position] // shards_of).reshape((-1,) + (1,) * (len(extent) - position - 1))

    level = one(*cuts[0])
    for cut in cuts[1:]:
        level = level * one(*cut)
    return level


def scatter_about(rng, dims, scale, bound, cuts=(), held_as=jnp.bfloat16):
    drawn = jax.random.normal(rng, dims, jnp.float32) * scale
    if len(cuts) > 0:
        drawn = block_scale(rng, dims, cuts, -0.22, 0.18) * drawn
    return jnp.clip(drawn, min=-bound, max=bound).astype(held_as)


def gaussian_with(key, extent, width, limit, shards, heavy, kind=jnp.bfloat16):
    result = width * jax.random.normal(key, extent, jnp.float32)
    if shards:
        result = result * block_scale(key, extent, shards, -0.22, 0.18)
    return jnp.clip(spiked(result, jax.random.fold_in(key, 3), *heavy), -limit, limit).astype(kind)


def setup_inputs(seed: int = 0) -> dict:
    keys = jax.random.split(jax.random.key(seed), 11)
    perturb = scatter_about(keys[0], (27, NX, NY, NZ), 1.0, 2.5, ((1, 2), (2, 4), (3, 4)), jnp.float32)
    density = jnp.clip(0.9 + 0.20000005 * jax.random.uniform(keys[1], (NX, NY, NZ), jnp.float32) ** block_scale(keys[1], (NX, NY, NZ), ((0, 2), (1, 4), (2, 4)), -0.2, 0.2), 0.9, 1.1)
    velocity = scatter_about(keys[2], (3, NX, NY, NZ), 0.04, 0.12, ((1, 2), (2, 4), (3, 4)), jnp.float32)
    excitation = jnp.clip(jnp.exp(math.log(0.2) - 7.6009025 * jax.random.uniform(keys[3], (NX, NY, NZ), jnp.float32) ** block_scale(keys[3], (NX, NY, NZ), ((0, 2), (1, 4), (2, 4)), -0.2, 0.2)), 0.0001, 0.2)
    solid_flag = plant((jax.random.randint(keys[4], (NX, NY, NZ), 0, 8) < 1).astype(jnp.int32), jax.random.fold_in(keys[4], 1), 0, 1)
    panel_cell = plant(jax.random.randint(keys[5], (SLOTS,), 0, BX * BY * BZ), jax.random.fold_in(keys[5], 1), 0, (BX * BY * BZ) - 1).astype(jnp.int32)
    panel_owner = draw_panel_owner(jax.random.fold_in(keys[10], 71), 0)
    panel_area = scatter_about(keys[7], (3, SLOTS), 1.0, 4.0, ((1, 32),), jnp.float32)
    weights = gaussian_with(keys[8], (4, ALLROWS, NOBS), 0.3, 1.796875, ((1, 32),), (1, 2, 32, 2.75))
    bin_offset = plant(jax.random.randint(keys[9], (TILES, NOBS // OTILE), 0, NB - STEPS + 1), jax.random.fold_in(keys[9], 1), 0, NB - STEPS).astype(jnp.int32)
    return {"perturb": perturb, "density": density, "velocity": velocity, "excitation": excitation, "solid_flag": solid_flag, "panel_cell": panel_cell, "panel_owner": panel_owner, "panel_area": panel_area, "weights": weights, "bin_offset": bin_offset}


beta_relax = 0.99
floor_level = 1e-6


def lattice():
    number = np.arange(27)
    step_x = number // 9 - 1
    step_y = (number // 3) % 3 - 1
    step_z = number % 3 - 1
    taxicab = np.abs(step_x) + np.abs(step_y) + np.abs(step_z)
    lattice_weight = np.array([8.0 / 27.0, 2.0 / 27.0, 1.0 / 54.0, 1.0 / 216.0])[taxicab]
    return step_x, step_y, step_z, lattice_weight


def tables():
    step_x, step_y, step_z, lattice_weight = lattice()
    mass_momentum = np.stack([np.ones(27), step_x, step_y, step_z])
    stress_rows = np.stack([step_x * step_x, step_y * step_y, step_z * step_z, step_x * step_y, step_x * step_z, step_y * step_z])
    shear_rows = np.stack([step_x * step_x, step_y * step_y, step_z * step_z, 2 * step_x * step_y, 2 * step_x * step_z, 2 * step_y * step_z])
    shear_table = (4.5 * lattice_weight)[:, None] * shear_rows.T
    return (jnp.asarray(mass_momentum, jnp.float32), jnp.asarray(stress_rows, jnp.float32),
            jnp.asarray(shear_table, jnp.float32), jnp.asarray(lattice_weight, jnp.float32))


def project(table, field):
    return jnp.tensordot(table, field, axes=1, precision=lax.Precision.HIGHEST)


def spread(vector, template):
    return vector.reshape((-1,) + (1,) * (template.ndim - 1))


def equilibrium(density, velocity):
    mass_momentum, stress_rows, shear_table, lattice_weight = tables()
    along = project(mass_momentum[1:].T, velocity)
    speed_sq = jnp.sum(velocity * velocity, axis=0)
    shaped = spread(lattice_weight, along)
    return shaped * density * (1.0 + 3.0 * along + 4.5 * along * along - 1.5 * speed_sq)


def collide(populations):
    mass_momentum, stress_rows, shear_table, lattice_weight = tables()
    moment_vals = project(mass_momentum, populations)
    density = moment_vals[0]
    velocity = moment_vals[1:] / density
    departure = populations - equilibrium(density, velocity)
    stress = project(stress_rows, departure)
    trace_third = (stress[0] + stress[1] + stress[2]) / 3.0
    deviator = jnp.concatenate([stress[:3] - trace_third, stress[3:]], axis=0)
    shear_part = project(shear_table, deviator)
    higher_part = departure - shear_part
    inverse_weight = spread(1.0 / lattice_weight, populations)
    cross_sum = jnp.sum(shear_part * higher_part * inverse_weight, axis=0)
    self_sum = jnp.maximum(jnp.sum(higher_part * higher_part * inverse_weight, axis=0), floor_level)
    stabilizer = 1.0 / beta_relax - (2.0 - 1.0 / beta_relax) * cross_sum / self_sum
    return populations - beta_relax * (2.0 * shear_part + stabilizer * higher_part)


def stream_periodic(star, solid_flag):
    step_x, step_y, step_z, lattice_weight = lattice()
    pieces = []
    for direction in range(27):
        offsets = (int(step_x[direction]), int(step_y[direction]), int(step_z[direction]))
        moved = jnp.roll(star[direction], offsets, axis=(0, 1, 2))
        wall = jnp.roll(solid_flag, offsets, axis=(0, 1, 2)) != 0
        pieces.append(jnp.where(wall, star[26 - direction], moved))
    return jnp.stack(pieces)


def measure(cell_pops, panel_area):
    mass_momentum, stress_rows, shear_table, lattice_weight = tables()
    moment_vals = project(mass_momentum, cell_pops)
    density = moment_vals[0]
    velocity = moment_vals[1:] / density
    pressure = (density - 1.0) / 3.0
    normal_flow = jnp.sum(velocity * panel_area, axis=0)
    mass_flux = density * normal_flow
    load_flux = pressure * panel_area + density * velocity * normal_flow
    return jnp.concatenate([mass_flux[None], load_flux], axis=0).astype(jnp.bfloat16)


def reference(perturb, density, velocity, excitation, solid_flag, panel_cell, panel_owner, panel_area, weights, bin_offset):
    populations = equilibrium(density, velocity) * (1.0 + excitation * perturb)
    slot_device = jnp.arange(SLOTS, dtype=jnp.int32) // PS
    device_x = slot_device // (N_GY * N_GZ)
    device_y = (slot_device // N_GZ) % N_GY
    device_z = slot_device % N_GZ
    global_x = device_x * BX + panel_cell // (BY * BZ)
    global_y = device_y * BY + (panel_cell // BZ) % BY
    global_z = device_z * BZ + panel_cell % BZ
    samples = []
    for step_index in range(STEPS):
        star = jnp.transpose(lax.map(collide, jnp.transpose(populations, (1, 0, 2, 3))), (1, 0, 2, 3))
        populations = stream_periodic(star, solid_flag)
        cell_pops = populations[:, global_x, global_y, global_z]
        samples.append(measure(cell_pops, panel_area))
    sampled = jnp.stack(samples, axis=1)
    owner_grid = panel_owner.reshape(DEVICES, PS)
    owner_hits = (owner_grid[:, :, None] == jnp.arange(GROUP, dtype=jnp.int32)[None, None, :]).astype(jnp.int32)
    slot_rank = jnp.sum(jnp.cumsum(owner_hits, axis=1) * owner_hits, axis=2) - 1
    sender = jnp.arange(DEVICES, dtype=jnp.int32)[:, None]
    target = (owner_grid * N_GZ + sender % N_GZ) * ROWS + (sender // N_GZ) * CAP + slot_rank
    received = jnp.zeros((4, STEPS, ALLROWS), jnp.bfloat16).at[:, :, target.reshape(-1).astype(jnp.int32)].set(sampled)
    tile_local = ROWS // PTILE
    offsets = jnp.repeat(bin_offset, OTILE, axis=1)
    shifts = jnp.arange(STEPS, dtype=jnp.int32)
    bins = jnp.arange(NB, dtype=jnp.int32)

    def owner_term(total, owner):
        start = (owner * ROWS).astype(jnp.int32)
        weight_block = lax.dynamic_slice_in_dim(weights, start, ROWS, 1).astype(jnp.float32)
        row_block = lax.dynamic_slice_in_dim(received, start, ROWS, 2).astype(jnp.float32)
        offset_block = lax.dynamic_slice_in_dim(offsets, (owner * tile_local).astype(jnp.int32), tile_local, 0)
        tiled = row_block.reshape(4, STEPS, tile_local, PTILE)
        grid_weights = weight_block.reshape(4, tile_local, PTILE, NOBS)
        summed = jnp.einsum("kstr,ktro->tso", tiled, grid_weights, precision=lax.Precision.HIGHEST)
        landing = (offset_block[:, None, :, None] + shifts[None, :, None, None] == bins[None, None, None, :]).astype(jnp.float32)
        partial_sum = jnp.einsum("tsob,tso->ob", landing, summed, precision=lax.Precision.HIGHEST)
        return total + partial_sum, None

    signal, unused = lax.scan(owner_term, jnp.zeros((NOBS, NB), jnp.float32), jnp.arange(DEVICES, dtype=jnp.int32))
    mass_momentum, stress_rows, shear_table, lattice_weight = tables()
    moment_vals = project(mass_momentum, populations)
    final_density = moment_vals[0]
    final_velocity = moment_vals[1:] / final_density
    wall = solid_flag != 0
    return jnp.where(wall, 1.0, final_density), jnp.where(wall[None], 0.0, final_velocity), signal
```

```python
import functools
import jax
import jax.numpy as jnp
import numpy as np
from jax import lax
from jax.experimental import pallas as pl
from jax.experimental.pallas import tpu as pltpu
from jax.sharding import PartitionSpec as P

STEPS = 4
NB = 128
BETA = 0.99
FLOOR = 1e-06
LANES = 128
ROWS = 160
FIRST = 16
TILES = 18
HALO_ROWS = 8 * TILES
HALO_TYPE = jnp.bfloat16
F32 = jnp.float32


VELS = [(i // 9 - 1, (i // 3) % 3 - 1, i % 3 - 1) for i in range(27)]
WEIGHT = [float([8 / 27, 2 / 27, 1 / 54, 1 / 216][sum(abs(a) for a in c)]) for c in VELS]


def pop(cx, cy, cz):
    return (cx + 1) * 9 + (cy + 1) * 3 + cz + 1


def x_place(cx, cy, cz):
    j = (cy + 1) * 3 + cz + 1
    if j < 8:
        return (0 if cx > 0 else 1), 16 * j
    return 2, (0 if cx > 0 else 64)


def x_flag_place(cx):
    return 2, (16 if cx > 0 else 80)


def y_slot(cx, cz):
    return (cx + 1) * 3 + cz + 1


def y_flag_slot(cx):
    return 9 + cx + 1


def lane_iota():
    return lax.broadcasted_iota(jnp.int32, (8, LANES), 1)


def turn(v, shift):
    shift %= LANES
    return v if shift == 0 else pltpu.roll(v, shift, 1)


def x_pattern(lane, a):
    out = jnp.zeros((8, LANES), F32)
    for cx in (1, -1):
        for cy in (-1, 0, 1):
            for cz in (-1, 0, 1):
                b, base = x_place(cx, cy, cz)
                if b == a:
                    out = jnp.where(lane // 16 == base // 16, WEIGHT[pop(cx, cy, cz)], out)
    return out


def y_pattern(lane):
    out = jnp.zeros((8, LANES), F32)
    for cx in (-1, 0, 1):
        for cz in (-1, 0, 1):
            out = jnp.where(lane % 16 == y_slot(cx, cz), WEIGHT[pop(cx, 1, cz)], out)
    return out


def moments(f):
    def total(vals):
        vals = list(vals)
        while len(vals) > 1:
            vals = [a + b for a, b in zip(vals[::2], vals[1::2])] + ([vals[-1]] if len(vals) % 2 else [])
        return vals[0]

    s = {}
    d = {}
    e = {}
    for cx in (-1, 0, 1):
        for cy in (-1, 0, 1):
            lo, mid, hi = f[pop(cx, cy, -1)], f[pop(cx, cy, 0)], f[pop(cx, cy, 1)]
            e[cx, cy] = lo + hi
            d[cx, cy] = hi - lo
            s[cx, cy] = mid + e[cx, cy]
    rows = {cx: s[cx, -1] + s[cx, 1] for cx in (-1, 0, 1)}
    full = {cx: rows[cx] + s[cx, 0] for cx in (-1, 0, 1)}
    dsum = {cx: d[cx, -1] + d[cx, 0] + d[cx, 1] for cx in (-1, 0, 1)}
    sxx = full[-1] + full[1]
    rho = sxx + full[0]
    jx = full[1] - full[-1]
    ydif = {cx: s[cx, 1] - s[cx, -1] for cx in (-1, 0, 1)}
    jy = ydif[-1] + ydif[0] + ydif[1]
    jz = dsum[-1] + dsum[0] + dsum[1]
    syy = rows[-1] + rows[0] + rows[1]
    szz = total([e[k] for k in e])
    sxy = ydif[1] - ydif[-1]
    sxz = dsum[1] - dsum[-1]
    syz = (d[-1, 1] + d[0, 1] + d[1, 1]) - (d[-1, -1] + d[0, -1] + d[1, -1])
    return rho, jx, jy, jz, sxx, syy, szz, sxy, sxz, syz


def collide(f, mom):
    rho, jx, jy, jz, sxx, syy, szz, sxy, sxz, syz = mom
    inv = 1.0 / rho
    ux, uy, uz = jx * inv, jy * inv, jz * inv
    pxx, pyy, pzz = sxx - jx * ux, syy - jy * uy, szz - jz * uz
    pxy, pxz, pyz = sxy - jx * uy, sxz - jx * uz, syz - jy * uz
    third = (pxx + pyy + pzz) * (1.0 / 3.0)
    qx, qy, qz = 4.5 * (pxx - third), 4.5 * (pyy - third), 4.5 * (pzz - third)
    qxy, qxz, qyz = 9.0 * pxy, 9.0 * pxz, 9.0 * pyz
    base = 1.0 - 1.5 * (ux * ux + uy * uy + uz * uz)
    rest = rho * base
    rho3 = 3.0 * rho
    rho45 = 4.5 * rho
    cross = None
    squares = {}
    higher = [None] * 27
    shear = [None] * 27
    for i in range(14):
        c = VELS[i]
        w = WEIGHT[i]
        cls = sum(abs(a) for a in c)
        if i == 13:
            h = f[13] - w * rest
            higher[13] = h
            squares[0] = h * h
            continue
        cu = None
        for a, u in zip(c, (ux, uy, uz)):
            if a:
                cu = (u if a > 0 else -u) if cu is None else (cu + u if a > 0 else cu - u)
        q = None
        for a, v in zip(c, (qx, qy, qz)):
            if a:
                q = v if q is None else q + v
        for a, b, v in ((c[0], c[1], qxy), (c[0], c[2], qxz), (c[1], c[2], qyz)):
            if a * b > 0:
                q = q + v
            elif a * b < 0:
                q = q - v
        even = w * (rest + rho45 * (cu * cu) + q)
        odd = (w * rho3) * cu
        hp = f[i] - even - odd
        hm = f[26 - i] - even + odd
        higher[i], higher[26 - i] = hp, hm
        shear[i] = shear[26 - i] = q
        term = q * (hp + hm)
        cross = term if cross is None else cross + term
        sq = hp * hp + hm * hm
        squares[cls] = sq if cls not in squares else squares[cls] + sq
    norm = squares[0] * (27.0 / 8.0) + squares[1] * 13.5 + squares[2] * 54.0 + squares[3] * 216.0
    gamma = 1.0 / BETA - (2.0 - 1.0 / BETA) * cross / jnp.maximum(norm, FLOOR)
    bg = BETA * gamma
    star = []
    for i in range(27):
        v = f[i] - bg * higher[i]
        if i != 13:
            v = v - (2.0 * BETA * WEIGHT[i]) * shear[i]
        star.append(v)
    return star, (rho, ux, uy, uz)


def pack(star, flag, lane, patterns):
    group = lane // 16
    slot = lane % 16
    xs = [jnp.zeros((8, LANES), F32) for _ in range(3)]
    for cx in (1, -1):
        source = 112 if cx > 0 else 0
        for cy in (-1, 0, 1):
            for cz in (-1, 0, 1):
                a, base = x_place(cx, cy, cz)
                xs[a] = jnp.where(group == base // 16, turn(star[pop(cx, cy, cz)], base - source), xs[a])
        if flag is not None:
            a, base = x_flag_place(cx)
            xs[a] = jnp.where(group == base // 16, turn(flag, base - source), xs[a])
    ys = []
    for cy in (1, -1):
        edge = 15 if cy > 0 else 0
        acc = jnp.zeros((8, LANES), F32)
        for cx in (-1, 0, 1):
            for cz in (-1, 0, 1):
                j = y_slot(cx, cz)
                acc = jnp.where(slot == j, turn(star[pop(cx, cy, cz)], 16 * cx + j - edge), acc)
            if flag is not None:
                j = y_flag_slot(cx)
                acc = jnp.where(slot == j, turn(flag, 16 * cx + j - edge), acc)
        ys.append(acc)
    return [v - p for v, p in zip(xs + ys, patterns)]


def all_patterns(lane):
    yp = y_pattern(lane)
    return [x_pattern(lane, 0), x_pattern(lane, 1), x_pattern(lane, 2), yp, yp]


def initial_kernel(perturb, density, velocity, excitation, solid, f_out, lo_out, hi_out, s_out):
    rho = density[...]
    ux, uy, uz = velocity[0], velocity[1], velocity[2]
    amplitude = excitation[...]
    base = 1.0 - 1.5 * (ux * ux + uy * uy + uz * uz)

    def put(i, v, out):
        out[FIRST : FIRST + 128, :] = v
        lo_out[4 * i : 4 * i + 4, :] = v[0:4, :]
        hi_out[4 * i : 4 * i + 4, :] = v[124:128, :]

    for i in range(27):
        c = VELS[i]
        shape = base
        cu = None
        for a, u in zip(c, (ux, uy, uz)):
            if a:
                cu = (u if a > 0 else -u) if cu is None else (cu + u if a > 0 else cu - u)
        if cu is not None:
            shape = shape + 3.0 * cu + 4.5 * (cu * cu)
        v = (WEIGHT[i] * rho) * shape * (1.0 + amplitude * perturb[i])
        put(i, v.T, f_out.at[i])
    put(27, solid[...].astype(F32).T, s_out)


def first_kernel(f_in, s_in, lo, hi, star_out, s_out, xp_out, yp_out, ym_out, edge, x_tmp, y_tmp):
    lane = lane_iota()
    patterns = all_patterns(lane)
    for i in range(28):
        below = lo[4 * i : 4 * i + 4, :]
        above = hi[4 * i : 4 * i + 4, :]
        edge[i, 0:4, :] = below
        edge[i, 4:8, :] = below
        edge[i, 8:12, :] = above
        edge[i, 12:16, :] = above

    def emit(t, load):
        f = [load(i) for i in range(27)]
        flag = load(27)
        star, unused = collide(f, moments(f))
        for i in range(27):
            star_out[i, pl.ds(8 * t, 8), :] = star[i]
        s_out[pl.ds(8 * t, 8), :] = flag
        packed = pack(star, flag, lane, patterns)
        row = 8 * t - 8
        for a in range(3):
            x_tmp[a, pl.ds(row, 8), :] = packed[a]
        y_tmp[0, pl.ds(row, 8), :] = packed[3]
        y_tmp[1, pl.ds(row, 8), :] = packed[4]

    def inner(k, carry):
        t = k + 2
        at = pl.ds(pl.multiple_of(8 * t, 8), 8)
        emit(t, lambda i: s_in[at, :] if i == 27 else f_in[i, at, :])
        return carry

    def outer(k, carry):
        at = pl.ds(pl.multiple_of(8 * k, 8), 8)
        emit(1 + 17 * k, lambda i: edge[i, at, :])
        return carry

    lax.fori_loop(0, 16, inner, 0)
    lax.fori_loop(0, 2, outer, 0)
    xp_out[...] = x_tmp[...].astype(xp_out.dtype)
    yp_out[...] = y_tmp[0].astype(yp_out.dtype)
    ym_out[...] = y_tmp[1].astype(ym_out.dtype)


def patch_kernel(with_flags, xh, yp_in, ym_in, yp_out, ym_out):
    lane = lax.broadcasted_iota(jnp.int32, (HALO_ROWS, LANES), 1)
    arrays = [xh[a].astype(F32) for a in range(3)]
    for cy, source, out in ((1, yp_in, yp_out), (-1, ym_in, ym_out)):
        y = 15 if cy > 0 else 0
        acc = source[...].astype(F32)
        for cx in (1, -1):
            col = 0 if cx > 0 else 112
            for cz in (-1, 0, 1):
                a, base = x_place(cx, cy, cz)
                j = y_slot(cx, cz)
                acc = jnp.where(lane == col + j, turn(arrays[a], col + j - base - y), acc)
            if with_flags:
                a, base = x_flag_place(cx)
                j = y_flag_slot(cx)
                acc = jnp.where(lane == col + j, turn(arrays[a], col + j - base - y), acc)
        out[...] = acc.astype(out.dtype)


def step_kernel(first, last, *refs):
    refs = list(refs)
    star_in, s_in, xh, yph, ymh = refs[:5]
    refs = refs[5:]
    if last:
        mom_out = refs.pop(0)
        star_out = None
    else:
        mom_out, star_out, xp_out, yp_out, ym_out = refs[:5]
        refs = refs[5:]
    if first:
        wall_ref = refs.pop(0)
    else:
        wall_ref = s_in
    xs, ys = refs[:2]
    lane = lane_iota()
    patterns = all_patterns(lane)
    slot = lane % 16
    halo = pl.ds(8, HALO_ROWS)

    def tall(v):
        return jnp.concatenate([v] * TILES, axis=0)

    for a in range(3):
        xs[a, halo, :] = xh[a].astype(F32) + tall(patterns[a])
    ys[0, halo, :] = yph[...].astype(F32) + tall(patterns[3])
    ys[1, halo, :] = ymh[...].astype(F32) + tall(patterns[4])
    edge_rows = (pl.ds(0, 8), pl.ds(ROWS - 8, 8))
    for at in edge_rows:
        for a in range(3):
            xs[a, at, :] = jnp.zeros((8, LANES), F32)
        for a in range(2):
            ys[a, at, :] = jnp.zeros((8, LANES), F32)
        if first:
            for k in range(9):
                wall_ref[k, at, :] = jnp.zeros((8, LANES), F32)

    def gather(v, cx, cy, x_at, x_load, y_slot_of, y_load):
        v = turn(v, 16 * cx + cy)
        if cx:
            a, base = x_at
            if cx > 0:
                v = jnp.where(lane < 16, turn(x_load(a), cy - base), v)
            else:
                v = jnp.where(lane >= 112, turn(x_load(a), 112 - base + cy), v)
        if cy > 0:
            v = jnp.where(slot == 0, turn(y_load(0), -y_slot_of), v)
        elif cy < 0:
            v = jnp.where(slot == 15, turn(y_load(1), 15 - y_slot_of), v)
        return v

    if first:
        def walls(k, carry):
            at = pl.ds(pl.multiple_of(8 * k + 8, 8), 8)
            flag = s_in[at, :]
            for cx in (-1, 0, 1):
                for cy in (-1, 0, 1):
                    wall_ref[(cx + 1) * 3 + cy + 1, at, :] = gather(
                        flag, cx, cy, x_flag_place(cx), lambda a: xs[a, at, :],
                        y_flag_slot(cx), lambda a: ys[a, at, :])
            return carry

        lax.fori_loop(0, TILES, walls, 0)

    def body(k, carry):
        t = k + 1
        here = pl.ds(pl.multiple_of(8 * t, 8), 8)
        own = [star_in[i, here, :] for i in range(27)]
        f = []
        for i in range(27):
            cx, cy, cz = VELS[i]
            at = here if cz == 0 else pl.ds(8 * t - cz, 8)
            v = own[i] if cz == 0 else star_in[i, at, :]
            v = gather(v, cx, cy, x_place(cx, cy, cz), lambda a: xs[a, at, :],
                       y_slot(cx, cz), lambda a: ys[a, at, :])
            if i != 13:
                wall = wall_ref[(cx + 1) * 3 + cy + 1, at, :]
                v = jnp.where(wall > 0.5, own[26 - i], v)
            else:
                v = own[13]
            f.append(v)
        mom = moments(f)
        row = pl.ds(pl.multiple_of(8 * k, 8), 8)
        if last:
            inv = 1.0 / mom[0]
            rho, ux, uy, uz = mom[0], mom[1] * inv, mom[2] * inv, mom[3] * inv
        else:
            star, (rho, ux, uy, uz) = collide(f, mom)
            for i in range(27):
                star_out[i, here, :] = star[i]
            packed = pack(star, None, lane, patterns)
            for a in range(3):
                xs_next[a, row, :] = packed[a]
            ys_next[0, row, :] = packed[3]
            ys_next[1, row, :] = packed[4]
        for a, v in enumerate((rho, ux, uy, uz)):
            mom_out[a, row, :] = v
        return carry

    if not last:
        xs_next, ys_next = refs[2:4]
    lax.fori_loop(0, TILES, body, 0)
    if not last:
        xp_out[...] = xs_next[...].astype(xp_out.dtype)
        yp_out[...] = ys_next[0].astype(yp_out.dtype)
        ym_out[...] = ys_next[1].astype(ym_out.dtype)


def prepare_kernel(capacity, owner_row, owner_col, cell, placing_out, lane_out, row_out):
    slots = owner_row.shape[1]
    q = lax.broadcasted_iota(jnp.int32, (slots, slots), 0)
    p = lax.broadcasted_iota(jnp.int32, (slots, slots), 1)
    same = (owner_row[...] == owner_col[...]) & (q < p)
    rank = jnp.sum(same.astype(F32), axis=0, keepdims=True).astype(jnp.int32)
    column = owner_row[...] * capacity + rank
    rows = placing_out.shape[0]
    placing_out[...] = (lax.broadcasted_iota(jnp.int32, (rows, slots), 0) == column).astype(F32).astype(jnp.bfloat16)
    k = lax.broadcasted_iota(jnp.int32, (LANES, slots), 0)
    lane_out[...] = (k == cell[...] // 128).astype(F32).astype(jnp.bfloat16)
    row_out[...] = (k == cell[...] % 128).astype(F32)


def split3(v):
    hi = v.astype(jnp.bfloat16)
    left = v - hi.astype(F32)
    mid = left.astype(jnp.bfloat16)
    low = (left - mid.astype(F32)).astype(jnp.bfloat16)
    return hi, mid, low


def sample_kernel(mom, lane_hot, row_hot, area, placing, out):
    fields = []
    hot = row_hot[...]
    lanes = lane_hot[...]
    for a in range(4):
        picked = None
        for part in split3(mom[a, 8 : 8 + 128, :]):
            term = jnp.dot(part, lanes, preferred_element_type=F32)
            picked = term if picked is None else picked + term
        fields.append(jnp.sum(picked * hot, axis=0, keepdims=True))
    rho, u = fields[0], fields[1:]
    pressure = (rho - 1.0) / 3.0
    normal = [area[j : j + 1, :] for j in range(3)]
    flow = u[0] * normal[0] + u[1] * normal[1] + u[2] * normal[2]
    rows = [rho * flow] + [pressure * normal[j] + rho * u[j] * flow for j in range(3)]
    stacked = jnp.concatenate(rows + [jnp.zeros_like(rho)] * 4, axis=0).astype(jnp.bfloat16)
    out[...] = lax.dot_general(stacked, placing[...], (((1,), (1,)), ((), ())), preferred_element_type=F32)


def scatter_kernel(groups, capacity, *refs):
    parts, out = refs[:-1], refs[-1]
    whole = jnp.concatenate([r[...] for r in parts], axis=0)
    for g in range(groups):
        out[g] = whole[:, g * capacity : (g + 1) * capacity].astype(out.dtype)


def observe_kernel(groups, capacity, ptile, rec, weights, offset, out):
    tiles = offset.shape[0]
    total = jnp.concatenate([rec[g].astype(F32) for g in range(groups)], axis=1)
    rows = total.shape[1]
    keep = lax.broadcasted_iota(jnp.int32, (tiles, rows), 1) // ptile == lax.broadcasted_iota(jnp.int32, (tiles, rows), 0)
    acc = None
    for k in range(4):
        left = [
            jnp.where(keep, jnp.broadcast_to(total[8 * s + k : 8 * s + k + 1, :], (tiles, rows)), 0.0)
            for s in range(STEPS)
        ]
        term = jnp.dot(jnp.concatenate(left, axis=0).astype(jnp.bfloat16), weights[k], preferred_element_type=F32)
        acc = term if acc is None else acc + term
    devices = out.shape[0]
    count = acc.shape[1] // devices
    obs_tile = acc.shape[1] // offset.shape[1]
    lane = lax.broadcasted_iota(jnp.int32, (tiles, LANES), 1)
    for d in range(devices):
        start = d * count
        piece = jnp.zeros((tiles, LANES), F32)
        for s in range(STEPS):
            block = acc[tiles * s : tiles * (s + 1), start // LANES * LANES : start // LANES * LANES + LANES]
            moved = turn(block, s * count - start % LANES)
            piece = jnp.where(lane // count == s, moved, piece)
        out[d, 0:tiles, :] = piece
        o = start // obs_tile
        out[d, tiles : 2 * tiles, :] = jnp.broadcast_to(offset[:, o : o + 1], (tiles, LANES))


def signal_kernel(got, mom, solid, out, density_out, velocity_out):
    devices, twice = got.shape[0], got.shape[1]
    tiles = twice // 2
    count = out.shape[0]
    values = got[:, 0:tiles, :].reshape(devices * tiles, LANES)
    start = got[:, tiles:twice, :].reshape(devices * tiles, LANES)
    bins = lax.broadcasted_iota(jnp.int32, (devices * tiles, NB), 1).astype(F32)
    parts = split3(values)
    total = None
    for s in range(STEPS):
        hot = (start + float(s) == bins).astype(F32).astype(jnp.bfloat16)
        acc = None
        for part in parts:
            term = lax.dot_general(part, hot, (((0,), (0,)), ((), ())), preferred_element_type=F32)
            acc = term if acc is None else acc + term
        acc = acc[s * count : (s + 1) * count, :]
        total = acc if total is None else total + acc
    out[...] = total
    wall = solid[...] != 0
    density_out[...] = jnp.where(wall, 1.0, mom[0, 8:136, :].T)
    for a in range(3):
        velocity_out[a] = jnp.where(wall, 0.0, mom[a + 1, 8:136, :].T)


def call(kernel, outs, *args, scratch=(), flops=1000000, limit=24):
    return pl.pallas_call(
        kernel,
        out_shape=outs,
        in_specs=[pl.BlockSpec(memory_space=pltpu.VMEM)] * len(args),
        out_specs=jax.tree.map(lambda _: pl.BlockSpec(memory_space=pltpu.VMEM), outs),
        scratch_shapes=list(scratch),
        compiler_params=pltpu.CompilerParams(vmem_limit_bytes=limit << 20),
        cost_estimate=pl.CostEstimate(
            flops=flops, transcendentals=0,
            bytes_accessed=sum(a.size * a.dtype.itemsize for a in args)),
    )(*args)


def ring(axis, shift):
    count = lax.axis_size(axis)
    return [(i, (i + shift) % count) for i in range(count)]


def exchange_x(xp):
    if lax.axis_size("gx") == 2:
        return lax.ppermute(xp, "gx", ring("gx", 1))
    low = lax.ppermute(jnp.stack([xp[0], xp[2]]), "gx", ring("gx", 1))
    high = lax.ppermute(jnp.stack([xp[1], xp[2]]), "gx", ring("gx", -1))
    mixed = jnp.where(jnp.arange(LANES) < 64, low[1], high[1])
    return jnp.stack([low[0], high[0], mixed])


def exchange(xp, yp, ym, with_flags):
    xh = exchange_x(xp)
    face = jax.ShapeDtypeStruct((HALO_ROWS, LANES), HALO_TYPE)
    yp, ym = call(functools.partial(patch_kernel, with_flags), (face, face), xh, yp, ym)
    return xh, lax.ppermute(yp, "gy", ring("gy", 1)), lax.ppermute(ym, "gy", ring("gy", -1))


def shards(perturb, density, velocity, excitation, solid_flag, panel_cell, panel_owner, panel_area, weights, bin_offset):
    bx, by, bz = density.shape
    assert bx * by == LANES and bz == LANES and by == 16
    flat = (LANES, LANES)
    solid = solid_flag.reshape(flat)
    block = jax.ShapeDtypeStruct((27, ROWS, LANES), F32)
    one = jax.ShapeDtypeStruct((ROWS, LANES), F32)
    rim = jax.ShapeDtypeStruct((28 * 4, LANES), F32)
    x_face = jax.ShapeDtypeStruct((3, HALO_ROWS, LANES), HALO_TYPE)
    y_face = jax.ShapeDtypeStruct((HALO_ROWS, LANES), HALO_TYPE)
    x_scratch = pltpu.VMEM((3, HALO_ROWS, LANES), F32)
    y_scratch = pltpu.VMEM((2, HALO_ROWS, LANES), F32)

    f0, low_rim, high_rim, flags = call(
        initial_kernel, (block, rim, rim, one),
        perturb.reshape((27,) + flat), density.reshape(flat), velocity.reshape((3,) + flat),
        excitation.reshape(flat), solid)
    below = lax.ppermute(high_rim, "gz", ring("gz", 1))
    above = lax.ppermute(low_rim, "gz", ring("gz", -1))

    group_count = lax.axis_size(("gx", "gy"))
    slots = panel_owner.shape[0]
    row_count = 2 * slots
    capacity = row_count // group_count
    placing, lane_hot, row_hot = call(
        functools.partial(prepare_kernel, capacity),
        (jax.ShapeDtypeStruct((row_count, slots), jnp.bfloat16),
         jax.ShapeDtypeStruct((LANES, slots), jnp.bfloat16),
         jax.ShapeDtypeStruct((LANES, slots), F32)),
        panel_owner.reshape(1, slots), panel_owner.reshape(slots, 1), panel_cell.reshape(1, slots))

    star, walls, xp, yp, ym = call(
        first_kernel, (block, one, x_face, y_face, y_face), f0, flags, below, above,
        scratch=(pltpu.VMEM((28, 16, LANES), F32), x_scratch, y_scratch))

    mom_shape = jax.ShapeDtypeStruct((4, HALO_ROWS, LANES), F32)
    routed = []
    for s in range(STEPS):
        first, last = s == 0, s == STEPS - 1
        xh, yph, ymh = exchange(xp, yp, ym, first)
        outs = [mom_shape]
        if not last:
            outs += [block, x_face, y_face, y_face]
        if first:
            outs += [jax.ShapeDtypeStruct((9, ROWS, LANES), F32)]
        scratch = [pltpu.VMEM((3, ROWS, LANES), F32), pltpu.VMEM((2, ROWS, LANES), F32)]
        if not last:
            scratch += [x_scratch, y_scratch]
        res = call(functools.partial(step_kernel, first, last), tuple(outs), star, walls, xh, yph, ymh, scratch=scratch)
        mom = res[0]
        if not last:
            star, xp, yp, ym = res[1:5]
        if first:
            walls = res[5]
        routed.append(call(sample_kernel, jax.ShapeDtypeStruct((8, row_count), F32),
                           mom, lane_hot, row_hot, panel_area, placing))

    sent = call(functools.partial(scatter_kernel, group_count, capacity),
                jax.ShapeDtypeStruct((group_count, 8 * STEPS, capacity), jnp.bfloat16), *routed)
    received = lax.all_to_all(sent, ("gx", "gy"), split_axis=0, concat_axis=0, tiled=True)

    tiles, obs_tiles = bin_offset.shape
    devices = lax.axis_size(("gx", "gy", "gz"))
    obs = weights.shape[2]
    count = obs // devices
    assert obs // obs_tiles % count == 0 and tiles % 8 == 0 and STEPS * count <= LANES
    observed = call(
        functools.partial(observe_kernel, group_count, capacity, row_count // tiles),
        jax.ShapeDtypeStruct((devices, 2 * tiles, LANES), F32),
        received, weights, bin_offset.astype(F32))
    got = lax.all_to_all(observed, ("gx", "gy", "gz"), split_axis=0, concat_axis=0, tiled=True)
    signal, final_density, final_velocity = call(
        signal_kernel,
        (jax.ShapeDtypeStruct((count, NB), F32), jax.ShapeDtypeStruct(flat, F32), jax.ShapeDtypeStruct((3,) + flat, F32)),
        got, mom, solid)
    return final_density.reshape(density.shape), final_velocity.reshape(velocity.shape), signal


def solution(mesh):
    cells = P("gx", "gy", "gz")
    vectors = P(None, "gx", "gy", "gz")
    every = ("gx", "gy", "gz")
    placed = (vectors, cells, vectors, cells, cells, P(every), P(every), P(None, every), P(None, every, None), P(every, None))
    return jax.shard_map(
        shards, mesh=mesh, in_specs=placed, out_specs=(cells, vectors, P(every, None)), check_vma=False)
```

```python
import functools
import jax
import jax.numpy as jnp
from jax import lax
from jax.experimental import pallas as pl
from jax.experimental.pallas import tpu as pltpu
from jax.sharding import PartitionSpec as P


STEPS = 4
NB = 128
BETA = 0.99
FLOOR = 1e-06
LANES = 128
ROWS = 160
FIRST = 16
TILES = 18
HALO_ROWS = 8 * TILES
HALO_TYPE = jnp.bfloat16
F32 = jnp.float32


VELS = [(i // 9 - 1, (i // 3) % 3 - 1, i % 3 - 1) for i in range(27)]
WEIGHT = [float([8 / 27, 2 / 27, 1 / 54, 1 / 216][sum(abs(a) for a in c)]) for c in VELS]


def pop(cx, cy, cz):
    return (cx + 1) * 9 + (cy + 1) * 3 + cz + 1


def x_place(cx, cy, cz):
    j = (cy + 1) * 3 + cz + 1
    if j < 8:
        return (0 if cx > 0 else 1), 16 * j
    return 2, (0 if cx > 0 else 64)


def x_flag_place(cx):
    return 2, (16 if cx > 0 else 80)


def y_slot(cx, cz):
    return (cx + 1) * 3 + cz + 1


def y_flag_slot(cx):
    return 9 + cx + 1


def lane_iota():
    return lax.broadcasted_iota(jnp.int32, (8, LANES), 1)


def turn(v, shift):
    shift %= LANES
    return v if shift == 0 else pltpu.roll(v, shift, 1)


def x_pattern(lane, a):
    out = jnp.zeros((8, LANES), F32)
    for cx in (1, -1):
        for cy in (-1, 0, 1):
            for cz in (-1, 0, 1):
                b, base = x_place(cx, cy, cz)
                if b == a:
                    out = jnp.where(lane // 16 == base // 16, WEIGHT[pop(cx, cy, cz)], out)
    return out


def y_pattern(lane):
    out = jnp.zeros((8, LANES), F32)
    for cx in (-1, 0, 1):
        for cz in (-1, 0, 1):
            out = jnp.where(lane % 16 == y_slot(cx, cz), WEIGHT[pop(cx, 1, cz)], out)
    return out


def moments(f):
    def total(vals):
        vals = list(vals)
        while len(vals) > 1:
            vals = [a + b for a, b in zip(vals[::2], vals[1::2])] + ([vals[-1]] if len(vals) % 2 else [])
        return vals[0]

    s = {}
    d = {}
    e = {}
    for cx in (-1, 0, 1):
        for cy in (-1, 0, 1):
            lo, mid, hi = f[pop(cx, cy, -1)], f[pop(cx, cy, 0)], f[pop(cx, cy, 1)]
            e[cx, cy] = lo + hi
            d[cx, cy] = hi - lo
            s[cx, cy] = mid + e[cx, cy]
    rows = {cx: s[cx, -1] + s[cx, 1] for cx in (-1, 0, 1)}
    full = {cx: rows[cx] + s[cx, 0] for cx in (-1, 0, 1)}
    dsum = {cx: d[cx, -1] + d[cx, 0] + d[cx, 1] for cx in (-1, 0, 1)}
    sxx = full[-1] + full[1]
    rho = sxx + full[0]
    jx = full[1] - full[-1]
    ydif = {cx: s[cx, 1] - s[cx, -1] for cx in (-1, 0, 1)}
    jy = ydif[-1] + ydif[0] + ydif[1]
    jz = dsum[-1] + dsum[0] + dsum[1]
    syy = rows[-1] + rows[0] + rows[1]
    szz = total([e[k] for k in e])
    sxy = ydif[1] - ydif[-1]
    sxz = dsum[1] - dsum[-1]
    syz = (d[-1, 1] + d[0, 1] + d[1, 1]) - (d[-1, -1] + d[0, -1] + d[1, -1])
    return rho, jx, jy, jz, sxx, syy, szz, sxy, sxz, syz


def collide(f, mom):
    rho, jx, jy, jz, sxx, syy, szz, sxy, sxz, syz = mom
    inv = 1.0 / rho
    ux, uy, uz = jx * inv, jy * inv, jz * inv
    pxx, pyy, pzz = sxx - jx * ux, syy - jy * uy, szz - jz * uz
    pxy, pxz, pyz = sxy - jx * uy, sxz - jx * uz, syz - jy * uz
    third = (pxx + pyy + pzz) * (1.0 / 3.0)
    qx, qy, qz = 4.5 * (pxx - third), 4.5 * (pyy - third), 4.5 * (pzz - third)
    qxy, qxz, qyz = 9.0 * pxy, 9.0 * pxz, 9.0 * pyz
    base = 1.0 - 1.5 * (ux * ux + uy * uy + uz * uz)
    rest = rho * base
    rho3 = 3.0 * rho
    rho45 = 4.5 * rho
    cross = None
    squares = {}
    higher = [None] * 27
    shear = [None] * 27
    for i in range(14):
        c = VELS[i]
        w = WEIGHT[i]
        cls = sum(abs(a) for a in c)
        if i == 13:
            h = f[13] - w * rest
            higher[13] = h
            squares[0] = h * h
            continue
        cu = None
        for a, u in zip(c, (ux, uy, uz)):
            if a:
                cu = (u if a > 0 else -u) if cu is None else (cu + u if a > 0 else cu - u)
        q = None
        for a, v in zip(c, (qx, qy, qz)):
            if a:
                q = v if q is None else q + v
        for a, b, v in ((c[0], c[1], qxy), (c[0], c[2], qxz), (c[1], c[2], qyz)):
            if a * b > 0:
                q = q + v
            elif a * b < 0:
                q = q - v
        even = w * (rest + rho45 * (cu * cu) + q)
        odd = (w * rho3) * cu
        hp = f[i] - even - odd
        hm = f[26 - i] - even + odd
        higher[i], higher[26 - i] = hp, hm
        shear[i] = shear[26 - i] = q
        term = q * (hp + hm)
        cross = term if cross is None else cross + term
        sq = hp * hp + hm * hm
        squares[cls] = sq if cls not in squares else squares[cls] + sq
    norm = squares[0] * (27.0 / 8.0) + squares[1] * 13.5 + squares[2] * 54.0 + squares[3] * 216.0
    gamma = 1.0 / BETA - (2.0 - 1.0 / BETA) * cross / jnp.maximum(norm, FLOOR)
    bg = BETA * gamma
    star = []
    for i in range(27):
        v = f[i] - bg * higher[i]
        if i != 13:
            v = v - (2.0 * BETA * WEIGHT[i]) * shear[i]
        star.append(v)
    return star, (rho, ux, uy, uz)


def pack(star, flag, lane, patterns):
    group = lane // 16
    slot = lane % 16
    xs = [jnp.zeros((8, LANES), F32) for _ in range(3)]
    for cx in (1, -1):
        source = 112 if cx > 0 else 0
        for cy in (-1, 0, 1):
            for cz in (-1, 0, 1):
                a, base = x_place(cx, cy, cz)
                xs[a] = jnp.where(group == base // 16, turn(star[pop(cx, cy, cz)], base - source), xs[a])
        if flag is not None:
            a, base = x_flag_place(cx)
            xs[a] = jnp.where(group == base // 16, turn(flag, base - source), xs[a])
    ys = []
    for cy in (1, -1):
        edge = 15 if cy > 0 else 0
        acc = jnp.zeros((8, LANES), F32)
        for cx in (-1, 0, 1):
            for cz in (-1, 0, 1):
                j = y_slot(cx, cz)
                acc = jnp.where(slot == j, turn(star[pop(cx, cy, cz)], 16 * cx + j - edge), acc)
            if flag is not None:
                j = y_flag_slot(cx)
                acc = jnp.where(slot == j, turn(flag, 16 * cx + j - edge), acc)
        ys.append(acc)
    return [v - p for v, p in zip(xs + ys, patterns)]


def corner_lanes(lane, cx):
    col = 0 if cx > 0 else 112
    slots = [y_slot(cx, cz) for cz in (-1, 0, 1)] + [y_flag_slot(cx)]
    out = lane == col + slots[0]
    for j in slots[1:]:
        out = out | (lane == col + j)
    return out


def corners(yp, ym):
    lane = lax.broadcasted_iota(jnp.int32, yp.shape, 1)
    up = corner_lanes(lane, 1) | corner_lanes(lane, -1)
    return jnp.where(up, yp, turn(ym, 16))


def all_patterns(lane):
    yp = y_pattern(lane)
    return [x_pattern(lane, 0), x_pattern(lane, 1), x_pattern(lane, 2), yp, yp]


def initial_kernel(perturb_hbm, density_hbm, velocity_hbm, excitation_hbm, solid_hbm, f_out, lo_out, hi_out, s_out,
                   perturb, density, velocity, excitation, solid, chunk_sem, sem):
    small = [
        pltpu.make_async_copy(src, dst, sem.at[k])
        for k, (src, dst) in enumerate(((density_hbm, density), (velocity_hbm, velocity),
                                        (excitation_hbm, excitation), (solid_hbm, solid)))
    ]
    for copy in small:
        copy.start()
    chunks = [
        pltpu.make_async_copy(perturb_hbm.at[pl.ds(3 * k, 3)], perturb.at[pl.ds(3 * k, 3)], chunk_sem.at[k])
        for k in range(9)
    ]
    for copy in chunks:
        copy.start()
    for copy in small:
        copy.wait()
    rho = density[...]
    ux, uy, uz = velocity[0], velocity[1], velocity[2]
    amplitude = excitation[...]
    base = 1.0 - 1.5 * (ux * ux + uy * uy + uz * uz)

    def put(i, v, out):
        out[FIRST : FIRST + 128, :] = v
        lo_out[4 * i : 4 * i + 4, :] = v[0:4, :]
        hi_out[4 * i : 4 * i + 4, :] = v[124:128, :]

    put(27, solid[...].astype(F32).T, s_out)
    for i in range(27):
        c = VELS[i]
        shape = base
        cu = None
        for a, u in zip(c, (ux, uy, uz)):
            if a:
                cu = (u if a > 0 else -u) if cu is None else (cu + u if a > 0 else cu - u)
        if cu is not None:
            shape = shape + 3.0 * cu + 4.5 * (cu * cu)
        if i % 3 == 0:
            chunks[i // 3].wait()
        v = (WEIGHT[i] * rho) * shape * (1.0 + amplitude * perturb[i])
        put(i, v.T, f_out.at[i])


def pack_tile(t, star_ref, flag_ref, lane, patterns, x_tmp, y_tmp):
    at = pl.ds(pl.multiple_of(8 * t, 8), 8)
    flag = None if flag_ref is None else flag_ref[at, :]
    packed = pack([star_ref[i, at, :] for i in range(27)], flag, lane, patterns)
    row = pl.ds(pl.multiple_of(8 * t - 8, 8), 8)
    for a in range(3):
        x_tmp[a, row, :] = packed[a]
    y_tmp[0, row, :] = packed[3]
    y_tmp[1, row, :] = packed[4]


def first_kernel(f_in, s_in, lo, hi, unused, star_out, s_out, xp_out, yp_out, ym_out, xc_out, edge, x_tmp, y_tmp):
    lane = lane_iota()
    patterns = all_patterns(lane)
    for i in range(28):
        below = lo[4 * i : 4 * i + 4, :]
        above = hi[4 * i : 4 * i + 4, :]
        edge[i, 0:4, :] = below
        edge[i, 4:8, :] = below
        edge[i, 8:12, :] = above
        edge[i, 12:16, :] = above

    def emit(t, load):
        f = [load(i) for i in range(27)]
        star, _ = collide(f, moments(f))
        at = pl.ds(pl.multiple_of(8 * t, 8), 8)
        for i in range(27):
            star_out[i, at, :] = star[i]
        s_out[at, :] = load(27)

    def pack_at(t):
        pack_tile(t, star_out, s_out, lane, patterns, x_tmp, y_tmp)

    def outer(k, carry):
        at = pl.ds(pl.multiple_of(8 * k, 8), 8)
        emit(1 + 17 * k, lambda i: edge[i, at, :])
        return carry

    def inner(k, carry):
        t = k + 2
        pack_at(t - 1)
        at = pl.ds(pl.multiple_of(8 * t, 8), 8)
        emit(t, lambda i: s_in[at, :] if i == 27 else f_in[i, at, :])
        return carry

    lax.fori_loop(0, 2, outer, 0)
    lax.fori_loop(0, 16, inner, 0)
    pack_at(17)
    pack_at(18)
    xp_out[...] = x_tmp[...].astype(xp_out.dtype)
    yp_out[...] = y_tmp[0].astype(yp_out.dtype)
    ym_out[...] = y_tmp[1].astype(ym_out.dtype)
    xc_out[...] = corners(y_tmp[0], y_tmp[1]).astype(xc_out.dtype)


def patch_kernel(low, high, yp_in, ym_in, yp_out, ym_out):
    lane = lax.broadcasted_iota(jnp.int32, (HALO_ROWS, LANES), 1)
    for shift, source, out in ((0, yp_in, yp_out), (-16, ym_in, ym_out)):
        acc = source[...].astype(F32)
        for cx, got in ((1, low), (-1, high)):
            acc = jnp.where(corner_lanes(lane, cx), turn(got[...].astype(F32), shift), acc)
        out[...] = acc.astype(out.dtype)


def step_kernel(first, last, *refs):
    refs = list(refs)
    star_in, s_in, xh, yph, ymh, _ = refs[:6]
    refs = refs[6:]
    if last:
        mom_out = refs.pop(0)
        star_out = None
    else:
        mom_out, star_out, xp_out, yp_out, ym_out, xc_out = refs[:6]
        refs = refs[6:]
    if first:
        wall_ref = refs.pop(0)
    else:
        wall_ref = s_in
    xs, ys = refs[:2]
    lane = lane_iota()
    patterns = all_patterns(lane)
    slot = lane % 16
    halo = pl.ds(8, HALO_ROWS)

    def tall(v):
        return jnp.concatenate([v] * TILES, axis=0)

    for a in range(3):
        xs[a, halo, :] = xh[a].astype(F32) + tall(patterns[a])
    ys[0, halo, :] = yph[...].astype(F32) + tall(patterns[3])
    ys[1, halo, :] = ymh[...].astype(F32) + tall(patterns[4])
    edge_rows = (pl.ds(0, 8), pl.ds(ROWS - 8, 8))
    for at in edge_rows:
        for a in range(3):
            xs[a, at, :] = jnp.zeros((8, LANES), F32)
        for a in range(2):
            ys[a, at, :] = jnp.zeros((8, LANES), F32)
        if first:
            for k in range(9):
                wall_ref[k, at, :] = jnp.zeros((8, LANES), F32)

    def gather(v, cx, cy, x_at, x_load, y_slot_of, y_load):
        v = turn(v, 16 * cx + cy)
        if cx:
            a, base = x_at
            if cx > 0:
                v = jnp.where(lane < 16, turn(x_load(a), cy - base), v)
            else:
                v = jnp.where(lane >= 112, turn(x_load(a), 112 - base + cy), v)
        if cy > 0:
            v = jnp.where(slot == 0, turn(y_load(0), -y_slot_of), v)
        elif cy < 0:
            v = jnp.where(slot == 15, turn(y_load(1), 15 - y_slot_of), v)
        return v

    if first:
        def walls(k, carry):
            at = pl.ds(pl.multiple_of(8 * k + 8, 8), 8)
            flag = s_in[at, :]
            for cx in (-1, 0, 1):
                for cy in (-1, 0, 1):
                    wall_ref[(cx + 1) * 3 + cy + 1, at, :] = gather(
                        flag, cx, cy, x_flag_place(cx), lambda a: xs[a, at, :],
                        y_flag_slot(cx), lambda a: ys[a, at, :])
            return carry

        lax.fori_loop(0, TILES, walls, 0)

    def gather_tile(t, buf):
        here = pl.ds(pl.multiple_of(8 * t, 8), 8)
        for i in range(27):
            cx, cy, cz = VELS[i]
            at = here if cz == 0 else pl.ds(8 * t - cz, 8)
            v = star_in[i, at, :]
            if i != 13:
                v = gather(v, cx, cy, x_place(cx, cy, cz), lambda a: xs[a, at, :],
                           y_slot(cx, cz), lambda a: ys[a, at, :])
                wall = wall_ref[(cx + 1) * 3 + cy + 1, at, :]
                v = jnp.where(wall > 0.5, star_in[26 - i, here, :], v)
            buf[i] = v

    def collide_tile(t, buf):
        f = [buf[i] for i in range(27)]
        mom = moments(f)
        if last:
            inv = 1.0 / mom[0]
            macro = mom[0], mom[1] * inv, mom[2] * inv, mom[3] * inv
        else:
            star, macro = collide(f, mom)
            here = pl.ds(pl.multiple_of(8 * t, 8), 8)
            for i in range(27):
                star_out[i, here, :] = star[i]
        row = pl.ds(pl.multiple_of(8 * t - 8, 8), 8)
        for a, v in enumerate(macro):
            mom_out[a, row, :] = v

    if not last:
        xs_next, ys_next = refs[2:4]
        refs = refs[2:]
    even, odd = refs[2:4]

    def pack_at(t):
        if not last:
            pack_tile(t, star_out, None, lane, patterns, xs_next, ys_next)

    def body(m, carry):
        pack_at(jnp.maximum(2 * m, 1))
        collide_tile(2 * m + 1, even)
        gather_tile(2 * m + 2, odd)
        pack_at(2 * m + 1)
        collide_tile(2 * m + 2, odd)
        gather_tile(jnp.minimum(2 * m + 3, TILES), even)
        return carry

    gather_tile(1, even)
    lax.fori_loop(0, TILES // 2, body, 0)
    pack_at(TILES)
    if not last:
        xp_out[...] = xs_next[...].astype(xp_out.dtype)
        yp_out[...] = ys_next[0].astype(yp_out.dtype)
        ym_out[...] = ys_next[1].astype(ym_out.dtype)
        xc_out[...] = corners(ys_next[0], ys_next[1]).astype(xc_out.dtype)


def prepare_kernel(capacity, owner_row, owner_col, cell, placing_out, lane_out, row_out):
    slots = owner_row.shape[1]
    q = lax.broadcasted_iota(jnp.int32, (slots, slots), 0)
    p = lax.broadcasted_iota(jnp.int32, (slots, slots), 1)
    same = (owner_row[...] == owner_col[...]) & (q < p)
    rank = jnp.sum(same.astype(F32), axis=0, keepdims=True).astype(jnp.int32)
    column = owner_row[...] * capacity + rank
    rows = placing_out.shape[0]
    placing_out[...] = (lax.broadcasted_iota(jnp.int32, (rows, slots), 0) == column).astype(F32).astype(jnp.bfloat16)
    k = lax.broadcasted_iota(jnp.int32, (LANES, slots), 0)
    lane_out[...] = (k == cell[...] // 128).astype(F32).astype(jnp.bfloat16)
    row_out[...] = (k == cell[...] % 128).astype(F32)


def split3(v):
    hi = v.astype(jnp.bfloat16)
    left = v - hi.astype(F32)
    mid = left.astype(jnp.bfloat16)
    low = (left - mid.astype(F32)).astype(jnp.bfloat16)
    return hi, mid, low


def sample_kernel(upper, mom, lane_hot, row_hot, area, placing, out):
    fields = []
    hot = row_hot[...]
    lanes = lane_hot[...]
    for a in range(4):
        picked = None
        for part in split3(mom[a, 8 : 8 + 128, :]):
            term = jnp.dot(part, lanes, preferred_element_type=F32)
            picked = term if picked is None else picked + term
        fields.append(jnp.sum(picked * hot, axis=0, keepdims=True))
    rho, u = fields[0], fields[1:]
    pressure = (rho - 1.0) / 3.0
    normal = [area[j : j + 1, :] for j in range(3)]
    flow = u[0] * normal[0] + u[1] * normal[1] + u[2] * normal[2]
    rows = [rho * flow] + [pressure * normal[j] + rho * u[j] * flow for j in range(3)]
    blank = [jnp.zeros_like(rho)] * 4
    stacked = jnp.concatenate(blank + rows if upper else rows + blank, axis=0).astype(jnp.bfloat16)
    out[...] = lax.dot_general(stacked, placing[...], (((1,), (1,)), ((), ())), preferred_element_type=F32)


def scatter_kernel(groups, capacity, *refs):
    parts, out = refs[:-1], refs[-1]
    pairs = [parts[0][...] + parts[1][...], parts[2][...] + parts[3][...]]
    lane = lane_iota()
    for g in range(groups):
        start = g * capacity
        tile = slice(start // LANES * LANES, start // LANES * LANES + LANES)
        low = turn(pairs[0][:, tile], -start)
        high = turn(pairs[1][:, tile], 64 - start)
        out[g] = jnp.where(lane < 64, low, high)


def window_kernel(solid_hbm, mom, unused, density_out, velocity_out, solid, sem):
    copy = pltpu.make_async_copy(solid_hbm, solid, sem.at[0])
    copy.start()
    copy.wait()
    wall = solid[...] != 0
    density_out[...] = jnp.where(wall, 1.0, mom[0, 8:136, :].T)
    for a in range(3):
        velocity_out[a] = jnp.where(wall, 0.0, mom[a + 1, 8:136, :].T)


def observe_kernel(groups, capacity, ptile, rec, weights_hbm, offset, out, weights, sem):
    obs = weights.shape[2]
    part = obs // 2
    copies = {}
    for h in range(2):
        for k in range(4):
            at = (k, slice(None), pl.ds(h * part, part))
            copies[h, k] = pltpu.make_async_copy(weights_hbm.at[at], weights.at[at], sem.at[4 * h + k])
            copies[h, k].start()
    tiles = offset.shape[0]
    rows = groups * capacity
    halves = []
    lane = lane_iota()
    per = LANES // capacity
    for half in range(2):
        pieces = []
        for start in range(0, groups, per):
            acc = jnp.zeros((8, LANES), F32)
            for g in range(start, start + per):
                moved = turn(rec[g], (g - start) * capacity - 64 * half)
                acc = jnp.where(lane // capacity == g - start, moved, acc)
            pieces.append(acc)
        halves.append(jnp.concatenate(pieces, axis=1))
    keep = lax.broadcasted_iota(jnp.int32, (tiles, rows), 1) // ptile == lax.broadcasted_iota(jnp.int32, (tiles, rows), 0)
    lefts = []
    for k in range(4):
        left = [
            jnp.where(keep, jnp.broadcast_to(halves[s // 2][4 * (s % 2) + k : 4 * (s % 2) + k + 1, :], (tiles, rows)), 0.0)
            for s in range(STEPS)
        ]
        lefts.append(jnp.concatenate(left, axis=0).astype(jnp.bfloat16))
    devices = out.shape[0]
    count = obs // devices
    obs_tile = obs // offset.shape[1]
    for h in range(2):
        acc = None
        for k in range(4):
            copies[h, k].wait()
            term = jnp.dot(lefts[k], weights[k, :, h * part : (h + 1) * part], preferred_element_type=F32)
            acc = term if acc is None else acc + term
        for d in range(h * devices // 2, (h + 1) * devices // 2):
            start = d * count
            here = start - h * part
            piece = jnp.zeros((tiles, LANES), F32)
            for s in range(STEPS):
                block = acc[tiles * s : tiles * (s + 1), here // LANES * LANES : here // LANES * LANES + LANES]
                moved = turn(block, s * count - start % LANES)
                piece = jnp.where(lane // count == s, moved, piece)
            out[d, 0:tiles, :] = piece
            o = start // obs_tile
            out[d, tiles : 2 * tiles, :] = jnp.broadcast_to(offset[:, o : o + 1], (tiles, LANES))


def signal_kernel(got, out):
    devices, twice = got.shape[0], got.shape[1]
    tiles = twice // 2
    count = out.shape[0]
    values = got[:, 0:tiles, :].reshape(devices * tiles, LANES)
    start = got[:, tiles:twice, :].reshape(devices * tiles, LANES)
    bins = lax.broadcasted_iota(jnp.int32, (devices * tiles, NB), 1).astype(F32)
    parts = split3(values)
    total = None
    for s in range(STEPS):
        hot = (start + float(s) == bins).astype(F32).astype(jnp.bfloat16)
        acc = None
        for part in parts:
            term = lax.dot_general(part, hot, (((0,), (0,)), ((), ())), preferred_element_type=F32)
            acc = term if acc is None else acc + term
        acc = acc[s * count : (s + 1) * count, :]
        total = acc if total is None else total + acc
    out[...] = total


def call(kernel, outs, *args, scratch=(), flops=1000000, limit=24, far=()):
    args = [pltpu.with_memory_space_constraint(a, pltpu.HBM) if k in far else a for k, a in enumerate(args)]
    return pl.pallas_call(
        kernel,
        out_shape=outs,
        in_specs=[pl.BlockSpec(memory_space=pltpu.HBM if k in far else pltpu.VMEM) for k in range(len(args))],
        out_specs=jax.tree.map(lambda _: pl.BlockSpec(memory_space=pltpu.VMEM), outs),
        scratch_shapes=list(scratch),
        compiler_params=pltpu.CompilerParams(vmem_limit_bytes=limit << 20),
        cost_estimate=pl.CostEstimate(
            flops=flops, transcendentals=0,
            bytes_accessed=sum(a.size * a.dtype.itemsize for a in args)),
    )(*args)


def ring(axis, shift):
    count = lax.axis_size(axis)
    return [(i, (i + shift) % count) for i in range(count)]


def shift(value, axis, by):
    return lax.ppermute(value, axis, ring(axis, by))


def exchange(xp, yp, ym, xc):
    if lax.axis_size("gx") == 2:
        low = high = shift(xc, "gx", 1)
        xh = shift(xp, "gx", 1)
    else:
        low = shift(xc, "gx", 1)
        high = shift(xc, "gx", -1)
        up = shift(jnp.stack([xp[0], xp[2]]), "gx", 1)
        down = shift(jnp.stack([xp[1], xp[2]]), "gx", -1)
        xh = jnp.stack([up[0], down[0], jnp.where(jnp.arange(LANES) < 64, up[1], down[1])])
    face = jax.ShapeDtypeStruct((HALO_ROWS, LANES), HALO_TYPE)
    yp, ym = call(patch_kernel, (face, face), low, high, yp, ym)
    return xh, shift(yp, "gy", 1), shift(ym, "gy", -1)


def shards(perturb, density, velocity, excitation, solid_flag, panel_cell, panel_owner, panel_area, weights, bin_offset):
    bx, by, bz = density.shape
    assert bx * by == LANES and bz == LANES and by == 16
    flat = (LANES, LANES)
    solid = solid_flag.reshape(flat)
    block = jax.ShapeDtypeStruct((27, ROWS, LANES), F32)
    one = jax.ShapeDtypeStruct((ROWS, LANES), F32)
    rim = jax.ShapeDtypeStruct((28 * 4, LANES), F32)
    x_face = jax.ShapeDtypeStruct((3, HALO_ROWS, LANES), HALO_TYPE)
    y_face = jax.ShapeDtypeStruct((HALO_ROWS, LANES), HALO_TYPE)
    x_scratch = pltpu.VMEM((3, HALO_ROWS, LANES), F32)
    y_scratch = pltpu.VMEM((2, HALO_ROWS, LANES), F32)

    f0, low_rim, high_rim, flags = call(
        initial_kernel, (block, rim, rim, one),
        perturb.reshape((27,) + flat), density.reshape(flat), velocity.reshape((3,) + flat),
        excitation.reshape(flat), solid,
        far=range(5),
        scratch=(pltpu.VMEM((27,) + flat, F32), pltpu.VMEM(flat, F32), pltpu.VMEM((3,) + flat, F32), pltpu.VMEM(flat, F32),
                 pltpu.VMEM(flat, jnp.int32), pltpu.SemaphoreType.DMA((9,)), pltpu.SemaphoreType.DMA((4,))))
    below = lax.ppermute(high_rim, "gz", ring("gz", 1))
    above = lax.ppermute(low_rim, "gz", ring("gz", -1))

    group_count = lax.axis_size(("gx", "gy"))
    slots = panel_owner.shape[0]
    row_count = 2 * slots
    capacity = row_count // group_count
    placing, lane_hot, row_hot = call(
        functools.partial(prepare_kernel, capacity),
        (jax.ShapeDtypeStruct((row_count, slots), jnp.bfloat16),
         jax.ShapeDtypeStruct((LANES, slots), jnp.bfloat16),
         jax.ShapeDtypeStruct((LANES, slots), F32)),
        panel_owner.reshape(1, slots), panel_owner.reshape(slots, 1), panel_cell.reshape(1, slots))

    star, walls, xp, yp, ym, xc = call(
        first_kernel, (block, one, x_face, y_face, y_face, y_face), f0, flags, below, above, placing,
        scratch=(pltpu.VMEM((28, 16, LANES), F32), x_scratch, y_scratch))

    mom_shape = jax.ShapeDtypeStruct((4, HALO_ROWS, LANES), F32)
    routed = []
    for s in range(STEPS):
        first, last = s == 0, s == STEPS - 1
        xh, yph, ymh = exchange(xp, yp, ym, xc)
        outs = [mom_shape]
        if not last:
            outs += [block, x_face, y_face, y_face, y_face]
        if first:
            outs += [jax.ShapeDtypeStruct((9, ROWS, LANES), F32)]
        scratch = [pltpu.VMEM((3, ROWS, LANES), F32), pltpu.VMEM((2, ROWS, LANES), F32)]
        if not last:
            scratch += [x_scratch, y_scratch]
        scratch += [pltpu.VMEM((27, 8, LANES), F32)] * 2
        res = call(functools.partial(step_kernel, first, last), tuple(outs), star, walls, xh, yph, ymh,
                   routed[-1] if routed else placing, scratch=scratch)
        mom = res[0]
        if not last:
            star, xp, yp, ym, xc = res[1:6]
        if first:
            walls = res[6]
        routed.append(call(functools.partial(sample_kernel, s % 2), jax.ShapeDtypeStruct((8, row_count), F32),
                           mom, lane_hot, row_hot, panel_area, placing))

    sent = call(functools.partial(scatter_kernel, group_count, capacity),
                jax.ShapeDtypeStruct((group_count, 8, LANES), F32), *routed)
    received = lax.all_to_all(sent, ("gx", "gy"), split_axis=0, concat_axis=0, tiled=True)

    final_density, final_velocity = call(
        window_kernel,
        (jax.ShapeDtypeStruct(flat, F32), jax.ShapeDtypeStruct((3,) + flat, F32)),
        solid, mom, sent, far=(0,), scratch=(pltpu.VMEM(flat, jnp.int32), pltpu.SemaphoreType.DMA((1,))))

    tiles, obs_tiles = bin_offset.shape
    devices = lax.axis_size(("gx", "gy", "gz"))
    obs = weights.shape[2]
    count = obs // devices
    assert obs // obs_tiles % count == 0 and tiles % 8 == 0 and STEPS * count <= LANES and capacity <= 64
    observed = call(
        functools.partial(observe_kernel, group_count, capacity, row_count // tiles),
        jax.ShapeDtypeStruct((devices, 2 * tiles, LANES), F32),
        received, weights, bin_offset.astype(F32), far=(1,),
        scratch=(pltpu.VMEM(weights.shape, weights.dtype), pltpu.SemaphoreType.DMA((8,))))
    got = lax.all_to_all(observed, ("gx", "gy", "gz"), split_axis=0, concat_axis=0, tiled=True)
    signal = call(signal_kernel, jax.ShapeDtypeStruct((count, NB), F32), got)
    return final_density.reshape(density.shape), final_velocity.reshape(velocity.shape), signal


def solution(mesh):
    cells = P("gx", "gy", "gz")
    vectors = P(None, "gx", "gy", "gz")
    every = ("gx", "gy", "gz")
    placed = (vectors, cells, vectors, cells, cells, P(every), P(every), P(None, every), P(None, every, None), P(every, None))
    return jax.shard_map(
        shards, mesh=mesh, in_specs=placed, out_specs=(cells, vectors, P(every, None)), check_vma=False)
```

```python
import functools
import jax
import jax.numpy as jnp
from jax import lax
from jax.experimental import pallas as pl
from jax.experimental.pallas import tpu as pltpu
from jax.sharding import PartitionSpec as P


STEPS = 4
NB = 128
BETA = 0.99
FLOOR = 1e-06
LANES = 128
ROWS = 160
FIRST = 16
TILES = 18
HALO_ROWS = 8 * TILES
HALO_TYPE = jnp.bfloat16
F32 = jnp.float32
TOP = 14.0


VELS = [(i // 9 - 1, (i // 3) % 3 - 1, i % 3 - 1) for i in range(27)]
WEIGHT = [float([8 / 27, 2 / 27, 1 / 54, 1 / 216][sum(abs(a) for a in c)]) for c in VELS]


def pop(cx, cy, cz):
    return (cx + 1) * 9 + (cy + 1) * 3 + cz + 1


def x_place(cx, cy, cz):
    j = (cy + 1) * 3 + cz + 1
    if j < 8:
        return (0 if cx > 0 else 1), 16 * j
    return 2, (0 if cx > 0 else 64)


def x_flag_place(cx):
    return 2, (16 if cx > 0 else 80)


def y_slot(cx, cz):
    return (cx + 1) * 3 + cz + 1


def y_flag_slot(cx):
    return 9 + cx + 1


def lane_iota():
    return lax.broadcasted_iota(jnp.int32, (8, LANES), 1)


def turn(v, shift):
    shift %= LANES
    return v if shift == 0 else pltpu.roll(v, shift, 1)


def x_pattern(lane, a):
    out = jnp.zeros((8, LANES), F32)
    for cx in (1, -1):
        for cy in (-1, 0, 1):
            for cz in (-1, 0, 1):
                b, base = x_place(cx, cy, cz)
                if b == a:
                    out = jnp.where(lane // 16 == base // 16, WEIGHT[pop(cx, cy, cz)], out)
    return out


def y_pattern(lane):
    out = jnp.zeros((8, LANES), F32)
    for cx in (-1, 0, 1):
        for cz in (-1, 0, 1):
            out = jnp.where(lane % 16 == y_slot(cx, cz), WEIGHT[pop(cx, 1, cz)], out)
    return out


def moments(f):
    def total(vals):
        vals = list(vals)
        while len(vals) > 1:
            vals = [a + b for a, b in zip(vals[::2], vals[1::2])] + ([vals[-1]] if len(vals) % 2 else [])
        return vals[0]

    s = {}
    d = {}
    e = {}
    for cx in (-1, 0, 1):
        for cy in (-1, 0, 1):
            lo, mid, hi = f[pop(cx, cy, -1)], f[pop(cx, cy, 0)], f[pop(cx, cy, 1)]
            e[cx, cy] = lo + hi
            d[cx, cy] = hi - lo
            s[cx, cy] = mid + e[cx, cy]
    rows = {cx: s[cx, -1] + s[cx, 1] for cx in (-1, 0, 1)}
    full = {cx: rows[cx] + s[cx, 0] for cx in (-1, 0, 1)}
    dsum = {cx: d[cx, -1] + d[cx, 0] + d[cx, 1] for cx in (-1, 0, 1)}
    sxx = full[-1] + full[1]
    rho = sxx + full[0]
    jx = full[1] - full[-1]
    ydif = {cx: s[cx, 1] - s[cx, -1] for cx in (-1, 0, 1)}
    jy = ydif[-1] + ydif[0] + ydif[1]
    jz = dsum[-1] + dsum[0] + dsum[1]
    syy = rows[-1] + rows[0] + rows[1]
    szz = total([e[k] for k in e])
    sxy = ydif[1] - ydif[-1]
    sxz = dsum[1] - dsum[-1]
    syz = (d[-1, 1] + d[0, 1] + d[1, 1]) - (d[-1, -1] + d[0, -1] + d[1, -1])
    return rho, jx, jy, jz, sxx, syy, szz, sxy, sxz, syz


def collide(f, mom):
    rho, jx, jy, jz, sxx, syy, szz, sxy, sxz, syz = mom
    inv = 1.0 / rho
    ux, uy, uz = jx * inv, jy * inv, jz * inv
    pxx, pyy, pzz = sxx - jx * ux, syy - jy * uy, szz - jz * uz
    pxy, pxz, pyz = sxy - jx * uy, sxz - jx * uz, syz - jy * uz
    third = (pxx + pyy + pzz) * (1.0 / 3.0)
    qx, qy, qz = 4.5 * (pxx - third), 4.5 * (pyy - third), 4.5 * (pzz - third)
    qxy, qxz, qyz = 9.0 * pxy, 9.0 * pxz, 9.0 * pyz
    base = 1.0 - 1.5 * (ux * ux + uy * uy + uz * uz)
    rest = rho * base
    rho3 = 3.0 * rho
    rho45 = 4.5 * rho
    cross = None
    squares = {}
    higher = [None] * 27
    shear = [None] * 27
    for i in range(14):
        c = VELS[i]
        w = WEIGHT[i]
        cls = sum(abs(a) for a in c)
        if i == 13:
            h = f[13] - w * rest
            higher[13] = h
            squares[0] = h * h
            continue
        cu = None
        for a, u in zip(c, (ux, uy, uz)):
            if a:
                cu = (u if a > 0 else -u) if cu is None else (cu + u if a > 0 else cu - u)
        q = None
        for a, v in zip(c, (qx, qy, qz)):
            if a:
                q = v if q is None else q + v
        for a, b, v in ((c[0], c[1], qxy), (c[0], c[2], qxz), (c[1], c[2], qyz)):
            if a * b > 0:
                q = q + v
            elif a * b < 0:
                q = q - v
        even = w * (rest + rho45 * (cu * cu) + q)
        odd = (w * rho3) * cu
        hp = f[i] - even - odd
        hm = f[26 - i] - even + odd
        higher[i], higher[26 - i] = hp, hm
        shear[i] = shear[26 - i] = q
        term = q * (hp + hm)
        cross = term if cross is None else cross + term
        sq = hp * hp + hm * hm
        squares[cls] = sq if cls not in squares else squares[cls] + sq
    norm = squares[0] * (27.0 / 8.0) + squares[1] * 13.5 + squares[2] * 54.0 + squares[3] * 216.0
    gamma = 1.0 / BETA - (2.0 - 1.0 / BETA) * cross / jnp.maximum(norm, FLOOR)
    bg = BETA * gamma
    star = []
    for i in range(27):
        v = f[i] - bg * higher[i]
        if i != 13:
            v = v - (2.0 * BETA * WEIGHT[i]) * shear[i]
        star.append(v)
    return star, (rho, ux, uy, uz)


def pack(star, flag, lane, patterns):
    group = lane // 16
    slot = lane % 16
    xs = [jnp.zeros((8, LANES), F32) for _ in range(3)]
    for cx in (1, -1):
        source = 112 if cx > 0 else 0
        for cy in (-1, 0, 1):
            for cz in (-1, 0, 1):
                a, base = x_place(cx, cy, cz)
                xs[a] = jnp.where(group == base // 16, turn(star[pop(cx, cy, cz)], base - source), xs[a])
        if flag is not None:
            a, base = x_flag_place(cx)
            xs[a] = jnp.where(group == base // 16, turn(flag, base - source), xs[a])
    ys = []
    for cy in (1, -1):
        edge = 15 if cy > 0 else 0
        acc = jnp.zeros((8, LANES), F32)
        for cx in (-1, 0, 1):
            for cz in (-1, 0, 1):
                j = y_slot(cx, cz)
                acc = jnp.where(slot == j, turn(star[pop(cx, cy, cz)], 16 * cx + j - edge), acc)
            if flag is not None:
                j = y_flag_slot(cx)
                acc = jnp.where(slot == j, turn(flag, 16 * cx + j - edge), acc)
        ys.append(acc)
    return [v - p for v, p in zip(xs + ys, patterns)]


FOLD = 48


def corner_lanes(lane, cx):
    col = 0 if cx > 0 else 112
    slots = [y_slot(cx, cz) for cz in (-1, 0, 1)] + [y_flag_slot(cx)]
    out = lane == col + slots[0]
    for j in slots[1:]:
        out = out | (lane == col + j)
    return out


def corners(yp, ym):
    lane = lax.broadcasted_iota(jnp.int32, yp.shape, 1)
    upper = corner_lanes(lane + 96, -1)
    lines = jnp.where(corner_lanes(lane, 1), yp, jnp.where(upper, turn(yp, -96), turn(ym, 16)))
    lane = lane[:FOLD]
    out = lines[:FOLD]
    for k in range(1, HALO_ROWS // FOLD):
        out = jnp.where(lane // 32 == k, turn(lines[k * FOLD : (k + 1) * FOLD], 32 * k), out)
    return out


def all_patterns(lane):
    yp = y_pattern(lane)
    return [x_pattern(lane, 0), x_pattern(lane, 1), x_pattern(lane, 2), yp, yp]


def initial_kernel(perturb_hbm, density_hbm, velocity_hbm, excitation_hbm, solid_hbm, f_out, lo_out, hi_out, s_out,
                   perturb, density, velocity, excitation, solid, chunk_sem, sem):
    small = [
        pltpu.make_async_copy(src, dst, sem.at[k])
        for k, (src, dst) in enumerate(((density_hbm, density), (velocity_hbm, velocity),
                                        (excitation_hbm, excitation), (solid_hbm, solid)))
    ]
    for copy in small:
        copy.start()
    chunks = [
        pltpu.make_async_copy(perturb_hbm.at[pl.ds(3 * k, 3)], perturb.at[pl.ds(3 * k, 3)], chunk_sem.at[k])
        for k in range(9)
    ]
    for copy in chunks:
        copy.start()
    for copy in small:
        copy.wait()
    rho = density[...]
    ux, uy, uz = velocity[0], velocity[1], velocity[2]
    amplitude = excitation[...]
    base = 1.0 - 1.5 * (ux * ux + uy * uy + uz * uz)

    def put(i, v, out):
        out[FIRST : FIRST + 128, :] = v
        lo_out[4 * i : 4 * i + 4, :] = v[0:4, :]
        hi_out[4 * i : 4 * i + 4, :] = v[124:128, :]

    put(27, solid[...].astype(F32).T, s_out)
    for i in range(27):
        c = VELS[i]
        shape = base
        cu = None
        for a, u in zip(c, (ux, uy, uz)):
            if a:
                cu = (u if a > 0 else -u) if cu is None else (cu + u if a > 0 else cu - u)
        if cu is not None:
            shape = shape + 3.0 * cu + 4.5 * (cu * cu)
        if i % 3 == 0:
            chunks[i // 3].wait()
        v = (WEIGHT[i] * rho) * shape * (1.0 + amplitude * perturb[i])
        put(i, v.T, f_out.at[i])


def pack_tile(t, star_ref, flag_ref, lane, patterns, x_tmp, y_tmp):
    at = pl.ds(pl.multiple_of(8 * t, 8), 8)
    flag = None if flag_ref is None else flag_ref[at, :]
    packed = pack([star_ref[i, at, :] for i in range(27)], flag, lane, patterns)
    row = pl.ds(pl.multiple_of(8 * t - 8, 8), 8)
    for a in range(3):
        x_tmp[a, row, :] = packed[a]
    y_tmp[0, row, :] = packed[3]
    y_tmp[1, row, :] = packed[4]


def first_kernel(f_in, s_in, lo, hi, unused, star_out, s_out, xp_out, yp_out, ym_out, xc_out, edge, x_tmp, y_tmp):
    lane = lane_iota()
    patterns = all_patterns(lane)
    for i in range(28):
        below = lo[4 * i : 4 * i + 4, :]
        above = hi[4 * i : 4 * i + 4, :]
        edge[i, 0:4, :] = below
        edge[i, 4:8, :] = below
        edge[i, 8:12, :] = above
        edge[i, 12:16, :] = above

    def emit(t, load):
        f = [load(i) for i in range(27)]
        star, _ = collide(f, moments(f))
        at = pl.ds(pl.multiple_of(8 * t, 8), 8)
        for i in range(27):
            star_out[i, at, :] = star[i]
        s_out[at, :] = load(27)

    def pack_at(t):
        pack_tile(t, star_out, s_out, lane, patterns, x_tmp, y_tmp)

    def outer(k, carry):
        at = pl.ds(pl.multiple_of(8 * k, 8), 8)
        emit(1 + 17 * k, lambda i: edge[i, at, :])
        return carry

    def inner(k, carry):
        t = k + 2
        pack_at(t - 1)
        at = pl.ds(pl.multiple_of(8 * t, 8), 8)
        emit(t, lambda i: s_in[at, :] if i == 27 else f_in[i, at, :])
        return carry

    lax.fori_loop(0, 2, outer, 0)
    lax.fori_loop(0, 16, inner, 0)
    pack_at(17)
    pack_at(18)
    xp_out[...] = x_tmp[...].astype(xp_out.dtype)
    yp_out[...] = y_tmp[0].astype(yp_out.dtype)
    ym_out[...] = y_tmp[1].astype(ym_out.dtype)
    xc_out[...] = corners(y_tmp[0], y_tmp[1]).astype(xc_out.dtype)


def patch_kernel(low, high, yp_in, ym_in, yp_out, ym_out):
    lane = lax.broadcasted_iota(jnp.int32, (FOLD, LANES), 1)
    got = {1: low[...].astype(F32), -1: high[...].astype(F32)}
    for shift, source, out in (({1: 0, -1: 96}, yp_in, yp_out), ({1: -16, -1: 112}, ym_in, ym_out)):
        for k in range(HALO_ROWS // FOLD):
            acc = source[k * FOLD : (k + 1) * FOLD, :].astype(F32)
            for cx in (1, -1):
                acc = jnp.where(corner_lanes(lane, cx), turn(got[cx], shift[cx] - 32 * k), acc)
            out[k * FOLD : (k + 1) * FOLD, :] = acc.astype(out.dtype)


def step_kernel(first, last, *refs):
    refs = list(refs)
    star_in, s_in, xh, yph, ymh, _ = refs[:6]
    refs = refs[6:]
    if last:
        mom_out = refs.pop(0)
        star_out = None
    else:
        mom_out, star_out, xp_out, yp_out, ym_out, xc_out = refs[:6]
        refs = refs[6:]
    if first:
        wall_ref = refs.pop(0)
    else:
        wall_ref = s_in
    xs, ys = refs[:2]
    lane = lane_iota()
    patterns = all_patterns(lane)
    slot = lane % 16
    halo = pl.ds(8, HALO_ROWS)

    def tall(v):
        return jnp.concatenate([v] * TILES, axis=0)

    for a in range(3):
        xs[a, halo, :] = xh[a].astype(F32) + tall(patterns[a])
    ys[0, halo, :] = yph[...].astype(F32) + tall(patterns[3])
    ys[1, halo, :] = ymh[...].astype(F32) + tall(patterns[4])
    edge_rows = (pl.ds(0, 8), pl.ds(ROWS - 8, 8))
    for at in edge_rows:
        for a in range(3):
            xs[a, at, :] = jnp.zeros((8, LANES), F32)
        for a in range(2):
            ys[a, at, :] = jnp.zeros((8, LANES), F32)
        if first:
            for k in range(9):
                wall_ref[k, at, :] = jnp.zeros((8, LANES), F32)

    def gather(v, cx, cy, x_at, x_load, y_slot_of, y_load):
        v = turn(v, 16 * cx + cy)
        if cx:
            a, base = x_at
            if cx > 0:
                v = jnp.where(lane < 16, turn(x_load(a), cy - base), v)
            else:
                v = jnp.where(lane >= 112, turn(x_load(a), 112 - base + cy), v)
        if cy > 0:
            v = jnp.where(slot == 0, turn(y_load(0), -y_slot_of), v)
        elif cy < 0:
            v = jnp.where(slot == 15, turn(y_load(1), 15 - y_slot_of), v)
        return v

    if first:
        def walls(k, carry):
            at = pl.ds(pl.multiple_of(8 * k + 8, 8), 8)
            flag = s_in[at, :]
            for cx in (-1, 0, 1):
                for cy in (-1, 0, 1):
                    wall_ref[(cx + 1) * 3 + cy + 1, at, :] = gather(
                        flag, cx, cy, x_flag_place(cx), lambda a: xs[a, at, :],
                        y_flag_slot(cx), lambda a: ys[a, at, :])
            return carry

        lax.fori_loop(0, TILES, walls, 0, unroll=6)

    def gather_tile(t, buf):
        here = pl.ds(pl.multiple_of(8 * t, 8), 8)
        for i in range(27):
            cx, cy, cz = VELS[i]
            at = here if cz == 0 else pl.ds(8 * t - cz, 8)
            v = star_in[i, at, :]
            if i != 13:
                v = gather(v, cx, cy, x_place(cx, cy, cz), lambda a: xs[a, at, :],
                           y_slot(cx, cz), lambda a: ys[a, at, :])
                wall = wall_ref[(cx + 1) * 3 + cy + 1, at, :]
                v = jnp.where(wall > 0.5, star_in[26 - i, here, :], v)
            buf[i] = v

    def collide_tile(t, buf):
        f = [buf[i] for i in range(27)]
        mom = moments(f)
        if last:
            inv = 1.0 / mom[0]
            macro = mom[0], mom[1] * inv, mom[2] * inv, mom[3] * inv
        else:
            star, macro = collide(f, mom)
            here = pl.ds(pl.multiple_of(8 * t, 8), 8)
            for i in range(27):
                star_out[i, here, :] = star[i]
        row = pl.ds(pl.multiple_of(8 * t - 8, 8), 8)
        for a, v in enumerate(macro):
            mom_out[a, row, :] = v

    if not last:
        xs_next, ys_next = refs[2:4]
        refs = refs[2:]
    even, odd = refs[2:4]

    def pack_at(t):
        if not last:
            pack_tile(t, star_out, None, lane, patterns, xs_next, ys_next)

    def body(m, carry):
        pack_at(jnp.maximum(2 * m, 1))
        collide_tile(2 * m + 1, even)
        gather_tile(2 * m + 2, odd)
        pack_at(2 * m + 1)
        collide_tile(2 * m + 2, odd)
        gather_tile(jnp.minimum(2 * m + 3, TILES), even)
        return carry

    gather_tile(1, even)
    lax.fori_loop(0, TILES // 2, body, 0)
    pack_at(TILES)
    if not last:
        xp_out[...] = xs_next[...].astype(xp_out.dtype)
        yp_out[...] = ys_next[0].astype(yp_out.dtype)
        ym_out[...] = ys_next[1].astype(ym_out.dtype)
        xc_out[...] = corners(ys_next[0], ys_next[1]).astype(xc_out.dtype)


def prepare_kernel(capacity, owner_row, owner_col, cell, placing_out, lane_out, row_out):
    slots = owner_row.shape[1]
    q = lax.broadcasted_iota(jnp.int32, (slots, slots), 0)
    p = lax.broadcasted_iota(jnp.int32, (slots, slots), 1)
    same = (owner_row[...] == owner_col[...]) & (q < p)
    rank = jnp.sum(same.astype(F32), axis=0, keepdims=True).astype(jnp.int32)
    column = owner_row[...] * capacity + rank
    rows = placing_out.shape[0]
    placing_out[...] = (lax.broadcasted_iota(jnp.int32, (rows, slots), 0) == column).astype(F32).astype(jnp.bfloat16)
    k = lax.broadcasted_iota(jnp.int32, (LANES, slots), 0)
    lane_out[...] = (k == cell[...] // 128).astype(F32).astype(jnp.bfloat16)
    row_out[...] = (k == cell[...] % 128).astype(F32)


def split3(v):
    hi = v.astype(jnp.bfloat16)
    left = v - hi.astype(F32)
    mid = left.astype(jnp.bfloat16)
    low = (left - mid.astype(F32)).astype(jnp.bfloat16)
    return hi, mid, low


def sample_rows(upper, mom, lane_hot, row_hot, area, placing):
    fields = []
    hot = row_hot[...]
    lanes = lane_hot[...]
    for a in range(4):
        picked = None
        for part in split3(mom[a, 8 : 8 + 128, :]):
            term = jnp.dot(part, lanes, preferred_element_type=F32)
            picked = term if picked is None else picked + term
        fields.append(jnp.sum(picked * hot, axis=0, keepdims=True))
    rho, u = fields[0], fields[1:]
    pressure = (rho - 1.0) / 3.0
    normal = [area[j : j + 1, :] for j in range(3)]
    flow = u[0] * normal[0] + u[1] * normal[1] + u[2] * normal[2]
    rows = [rho * flow] + [pressure * normal[j] + rho * u[j] * flow for j in range(3)]
    blank = [jnp.zeros_like(rho)] * 4
    stacked = jnp.concatenate(blank + rows if upper else rows + blank, axis=0).astype(jnp.bfloat16)
    return lax.dot_general(stacked, placing[...], (((1,), (1,)), ((), ())), preferred_element_type=F32)


def sample_kernel(upper, *refs):
    refs[-1][...] = sample_rows(upper, *refs[:-1])


def scatter_kernel(groups, capacity, mom, lane_hot, row_hot, area, placing, part0, part1, part2, out):
    last = sample_rows(1, mom, lane_hot, row_hot, area, placing)
    pairs = [part0[...] + part1[...], part2[...] + last]
    lane = lane_iota()
    for g in range(groups):
        start = g * capacity
        tile = slice(start // LANES * LANES, start // LANES * LANES + LANES)
        low = turn(pairs[0][:, tile], -start)
        high = turn(pairs[1][:, tile], 64 - start)
        value = jnp.where(lane < 64, low, high)
        out[g] = value


def fetch_kernel(weights_hbm, unused, out, sem):
    copy = pltpu.make_async_copy(weights_hbm.at[pl.ds(0, out.shape[0])], out, sem.at[0])
    copy.start()
    copy.wait()


def window_kernel(solid_hbm, mom, unused, density_out, velocity_out, solid, sem):
    copy = pltpu.make_async_copy(solid_hbm, solid, sem.at[0])
    copy.start()
    copy.wait()
    wall = solid[...] != 0
    density_out[...] = jnp.where(wall, 1.0, mom[0, 8:136, :].T)
    for a in range(3):
        velocity_out[a] = jnp.where(wall, 0.0, mom[a + 1, 8:136, :].T)


def observe_kernel(groups, capacity, ptile, weights_hbm, near, offset, rec, out_hbm, rest, out, sem):
    ahead = near.shape[0]
    copy = pltpu.make_async_copy(weights_hbm.at[pl.ds(ahead, 4 - ahead)], rest, sem.at[0])
    copy.start()
    obs = rest.shape[2]
    part = obs // 2
    tiles = offset.shape[0]
    rows = groups * capacity
    halves = []
    lane = lane_iota()
    per = LANES // capacity
    for half in range(2):
        pieces = []
        for start in range(0, groups, per):
            acc = jnp.zeros((8, LANES), F32)
            for g in range(start, start + per):
                moved = turn(rec[g], (g - start) * capacity - 64 * half)
                acc = jnp.where(lane // capacity == g - start, moved, acc)
            pieces.append(acc)
        halves.append(jnp.concatenate(pieces, axis=1))
    keep = lax.broadcasted_iota(jnp.int32, (tiles, rows), 1) // ptile == lax.broadcasted_iota(jnp.int32, (tiles, rows), 0)
    lefts = []
    for k in range(4):
        left = [
            jnp.where(keep, jnp.broadcast_to(halves[s // 2][4 * (s % 2) + k : 4 * (s % 2) + k + 1, :], (tiles, rows)), 0.0)
            for s in range(STEPS)
        ]
        lefts.append(jnp.concatenate(left, axis=0).astype(jnp.bfloat16))
    devices = out.shape[0]
    count = obs // devices
    obs_tile = obs // offset.shape[1]
    stores = []
    for h in range(2):
        acc = None
        for k in range(4):
            if k == ahead and h == 0:
                copy.wait()
            cols = slice(h * part, (h + 1) * part)
            right = near[k, :, cols] if k < ahead else rest[k - ahead, :, cols]
            term = jnp.dot(lefts[k], right, preferred_element_type=F32)
            acc = term if acc is None else acc + term
        peak = jnp.max(jnp.max(jnp.abs(acc), axis=1, keepdims=True), axis=0, keepdims=True)
        power = jnp.broadcast_to(jnp.ceil(jnp.log2(jnp.maximum(peak, 1e-30))), (tiles, LANES))
        down = jnp.exp2(TOP - power)
        for d in range(h * devices // 2, (h + 1) * devices // 2):
            start = d * count
            here = start - h * part
            piece = jnp.zeros((tiles, LANES), F32)
            for s in range(STEPS):
                block = acc[tiles * s : tiles * (s + 1), here // LANES * LANES : here // LANES * LANES + LANES]
                moved = turn(block, s * count - start % LANES)
                piece = jnp.where(lane // count == s, moved, piece)
            out[d, 0:tiles, :] = piece * down
            o = start // obs_tile
            out[d, tiles : 2 * tiles, :] = jnp.where(lane < 64, jnp.broadcast_to(offset[:, o : o + 1], (tiles, LANES)), power)
        half = pl.ds(h * (devices // 2), devices // 2)
        stores.append(pltpu.make_async_copy(out.at[half], out_hbm.at[half], sem.at[1 + h]))
        stores[h].start()
    for store in stores:
        store.wait()


def signal_kernel(got, out):
    devices, twice = got.shape[0], got.shape[1]
    tiles = twice // 2
    count = out.shape[0]
    shape = (devices * tiles, LANES)
    notes = got[:, tiles:twice, :].reshape(shape)
    start = jnp.broadcast_to(notes[:, 0:1], shape)
    values = got[:, 0:tiles, :].reshape(shape) * jnp.exp2(jnp.broadcast_to(notes[:, 64:65], shape) - TOP)
    bins = lax.broadcasted_iota(jnp.int32, (devices * tiles, NB), 1).astype(F32)
    hot = (start == bins).astype(F32).astype(jnp.bfloat16)
    acc = None
    for part in split3(values):
        term = lax.dot_general(part, hot, (((0,), (0,)), ((), ())), preferred_element_type=F32)
        acc = term if acc is None else acc + term
    total = None
    for s in range(STEPS):
        moved = turn(acc[s * count : (s + 1) * count, :], s)
        total = moved if total is None else total + moved
    out[...] = total


def call(kernel, outs, *args, scratch=(), flops=1000000, limit=24, far=()):
    args = [pltpu.with_memory_space_constraint(a, pltpu.HBM) if k in far else a for k, a in enumerate(args)]
    return pl.pallas_call(
        kernel,
        out_shape=outs,
        in_specs=[pl.BlockSpec(memory_space=pltpu.HBM if k in far else pltpu.VMEM) for k in range(len(args))],
        out_specs=jax.tree.map(lambda _: pl.BlockSpec(memory_space=pltpu.VMEM), outs),
        scratch_shapes=list(scratch),
        compiler_params=pltpu.CompilerParams(vmem_limit_bytes=limit << 20),
        cost_estimate=pl.CostEstimate(
            flops=flops, transcendentals=0,
            bytes_accessed=sum(a.size * a.dtype.itemsize for a in args)),
    )(*args)


def ring(axis, shift):
    count = lax.axis_size(axis)
    return [(i, (i + shift) % count) for i in range(count)]


def shift(value, axis, by):
    return lax.ppermute(value, axis, ring(axis, by))


def exchange(xp, yp, ym, xc):
    if lax.axis_size("gx") == 2:
        low = high = shift(xc, "gx", 1)
        xh = shift(xp, "gx", 1)
    else:
        low = shift(xc, "gx", 1)
        high = shift(xc, "gx", -1)
        up = shift(jnp.stack([xp[0], xp[2]]), "gx", 1)
        down = shift(jnp.stack([xp[1], xp[2]]), "gx", -1)
        xh = jnp.stack([up[0], down[0], jnp.where(jnp.arange(LANES) < 64, up[1], down[1])])
    face = jax.ShapeDtypeStruct((HALO_ROWS, LANES), HALO_TYPE)
    yp, ym = call(patch_kernel, (face, face), low, high, yp, ym)
    return xh, shift(yp, "gy", 1), shift(ym, "gy", -1)


def shards(perturb, density, velocity, excitation, solid_flag, panel_cell, panel_owner, panel_area, weights, bin_offset):
    bx, by, bz = density.shape
    assert bx * by == LANES and bz == LANES and by == 16
    flat = (LANES, LANES)
    solid = solid_flag.reshape(flat)
    block = jax.ShapeDtypeStruct((27, ROWS, LANES), F32)
    one = jax.ShapeDtypeStruct((ROWS, LANES), F32)
    rim = jax.ShapeDtypeStruct((28 * 4, LANES), F32)
    x_face = jax.ShapeDtypeStruct((3, HALO_ROWS, LANES), HALO_TYPE)
    y_face = jax.ShapeDtypeStruct((HALO_ROWS, LANES), HALO_TYPE)
    x_edge = jax.ShapeDtypeStruct((FOLD, LANES), HALO_TYPE)
    x_scratch = pltpu.VMEM((3, HALO_ROWS, LANES), F32)
    y_scratch = pltpu.VMEM((2, HALO_ROWS, LANES), F32)

    f0, low_rim, high_rim, flags = call(
        initial_kernel, (block, rim, rim, one),
        perturb.reshape((27,) + flat), density.reshape(flat), velocity.reshape((3,) + flat),
        excitation.reshape(flat), solid,
        far=range(5),
        scratch=(pltpu.VMEM((27,) + flat, F32), pltpu.VMEM(flat, F32), pltpu.VMEM((3,) + flat, F32), pltpu.VMEM(flat, F32),
                 pltpu.VMEM(flat, jnp.int32), pltpu.SemaphoreType.DMA((9,)), pltpu.SemaphoreType.DMA((4,))))
    below = lax.ppermute(high_rim, "gz", ring("gz", 1))
    above = lax.ppermute(low_rim, "gz", ring("gz", -1))

    group_count = lax.axis_size(("gx", "gy"))
    slots = panel_owner.shape[0]
    row_count = 2 * slots
    capacity = row_count // group_count
    placing, lane_hot, row_hot = call(
        functools.partial(prepare_kernel, capacity),
        (jax.ShapeDtypeStruct((row_count, slots), jnp.bfloat16),
         jax.ShapeDtypeStruct((LANES, slots), jnp.bfloat16),
         jax.ShapeDtypeStruct((LANES, slots), F32)),
        panel_owner.reshape(1, slots), panel_owner.reshape(slots, 1), panel_cell.reshape(1, slots))

    star, walls, xp, yp, ym, xc = call(
        first_kernel, (block, one, x_face, y_face, y_face, x_edge), f0, flags, below, above, placing,
        scratch=(pltpu.VMEM((28, 16, LANES), F32), x_scratch, y_scratch))

    mom_shape = jax.ShapeDtypeStruct((4, HALO_ROWS, LANES), F32)
    routed = []
    for s in range(STEPS):
        first, last = s == 0, s == STEPS - 1
        xh, yph, ymh = exchange(xp, yp, ym, xc)
        outs = [mom_shape]
        if not last:
            outs += [block, x_face, y_face, y_face, x_edge]
        if first:
            outs += [jax.ShapeDtypeStruct((9, ROWS, LANES), F32)]
        scratch = [pltpu.VMEM((3, ROWS, LANES), F32), pltpu.VMEM((2, ROWS, LANES), F32)]
        if not last:
            scratch += [x_scratch, y_scratch]
        scratch += [pltpu.VMEM((27, 8, LANES), F32)] * 2
        res = call(functools.partial(step_kernel, first, last), tuple(outs), star, walls, xh, yph, ymh,
                   routed[-1] if routed else placing, scratch=scratch)
        mom = res[0]
        if not last:
            star, xp, yp, ym, xc = res[1:6]
        if first:
            walls = res[6]
        if not last:
            routed.append(call(functools.partial(sample_kernel, s % 2), jax.ShapeDtypeStruct((8, row_count), F32),
                               mom, lane_hot, row_hot, panel_area, placing))

    send = functools.partial(scatter_kernel, group_count, capacity)
    samples = (mom, lane_hot, row_hot, panel_area, placing, *routed)

    def fetch(count, after):
        return call(fetch_kernel,
                    jax.ShapeDtypeStruct((count,) + weights.shape[1:], weights.dtype), weights, after, far=(0,),
                    scratch=(pltpu.SemaphoreType.DMA((1,)),))

    sent = call(send, jax.ShapeDtypeStruct((group_count, 8, LANES), F32), *samples)
    received = lax.all_to_all(sent, ("gx", "gy"), split_axis=0, concat_axis=0, tiled=True)
    near = fetch(3, sent)

    tiles, obs_tiles = bin_offset.shape
    devices = lax.axis_size(("gx", "gy", "gz"))
    obs = weights.shape[2]
    count = obs // devices
    assert obs // obs_tiles % count == 0 and tiles % 8 == 0 and STEPS * count <= LANES and capacity <= 64
    out_shape = (devices, 2 * tiles, LANES)
    observed = pl.pallas_call(
        functools.partial(observe_kernel, group_count, capacity, row_count // tiles),
        out_shape=jax.ShapeDtypeStruct(out_shape, F32),
        in_specs=[pl.BlockSpec(memory_space=pltpu.HBM)] + [pl.BlockSpec(memory_space=pltpu.VMEM)] * 3,
        out_specs=pl.BlockSpec(memory_space=pltpu.HBM),
        scratch_shapes=[pltpu.VMEM((4 - near.shape[0],) + weights.shape[1:], weights.dtype), pltpu.VMEM(out_shape, F32),
                        pltpu.SemaphoreType.DMA((3,))],
        compiler_params=pltpu.CompilerParams(vmem_limit_bytes=24 << 20),
    )(pltpu.with_memory_space_constraint(weights, pltpu.HBM), near, bin_offset.astype(F32), received)
    final_density, final_velocity = call(
        window_kernel,
        (jax.ShapeDtypeStruct(flat, F32), jax.ShapeDtypeStruct((3,) + flat, F32)),
        solid, mom, sent, far=(0,), scratch=(pltpu.VMEM(flat, jnp.int32), pltpu.SemaphoreType.DMA((1,))))
    got = lax.all_to_all(observed.astype(jnp.float16), ("gx", "gy", "gz"), split_axis=0, concat_axis=0, tiled=True)
    signal = call(signal_kernel, jax.ShapeDtypeStruct((count, NB), F32), got.astype(F32))
    return final_density.reshape(density.shape), final_velocity.reshape(velocity.shape), signal


def solution(mesh):
    cells = P("gx", "gy", "gz")
    vectors = P(None, "gx", "gy", "gz")
    every = ("gx", "gy", "gz")
    placed = (vectors, cells, vectors, cells, cells, P(every), P(every), P(None, every), P(None, every, None), P(every, None))
    return jax.shard_map(
        shards, mesh=mesh, in_specs=placed, out_specs=(cells, vectors, P(every, None)), check_vma=False)
```

```python
import functools
import jax
import jax.numpy as jnp
from jax import lax
from jax.experimental import pallas as pl
from jax.experimental.pallas import tpu as pltpu
from jax.sharding import PartitionSpec as P


STEPS = 4
NB = 128
BETA = 0.99
FLOOR = 1e-06
LANES = 128
ROWS = 160
FIRST = 16
TILES = 18
HALO_ROWS = 8 * TILES
HALO_TYPE = jnp.bfloat16
F32 = jnp.float32
TOP = 14.0


VELS = [(i // 9 - 1, (i // 3) % 3 - 1, i % 3 - 1) for i in range(27)]
WEIGHT = [float([8 / 27, 2 / 27, 1 / 54, 1 / 216][sum(abs(a) for a in c)]) for c in VELS]


def pop(cx, cy, cz):
    return (cx + 1) * 9 + (cy + 1) * 3 + cz + 1


def x_place(cx, cy, cz):
    j = (cy + 1) * 3 + cz + 1
    if j < 8:
        return (0 if cx > 0 else 1), 16 * j
    return 2, (0 if cx > 0 else 64)


def x_flag_place(cx):
    return 2, (16 if cx > 0 else 80)


def y_slot(cx, cz):
    return (cx + 1) * 3 + cz + 1


def y_flag_slot(cx):
    return 9 + cx + 1


def lane_iota():
    return lax.broadcasted_iota(jnp.int32, (8, LANES), 1)


def turn(v, shift):
    shift %= LANES
    return v if shift == 0 else pltpu.roll(v, shift, 1)


def moments(f):
    def total(vals):
        vals = list(vals)
        while len(vals) > 1:
            vals = [a + b for a, b in zip(vals[::2], vals[1::2])] + ([vals[-1]] if len(vals) % 2 else [])
        return vals[0]

    s = {}
    d = {}
    e = {}
    for cx in (-1, 0, 1):
        for cy in (-1, 0, 1):
            lo, mid, hi = f[pop(cx, cy, -1)], f[pop(cx, cy, 0)], f[pop(cx, cy, 1)]
            e[cx, cy] = lo + hi
            d[cx, cy] = hi - lo
            s[cx, cy] = mid + e[cx, cy]
    rows = {cx: s[cx, -1] + s[cx, 1] for cx in (-1, 0, 1)}
    full = {cx: rows[cx] + s[cx, 0] for cx in (-1, 0, 1)}
    dsum = {cx: d[cx, -1] + d[cx, 0] + d[cx, 1] for cx in (-1, 0, 1)}
    sxx = full[-1] + full[1]
    rho = 1.0 + (sxx + full[0])
    jx = full[1] - full[-1]
    ydif = {cx: s[cx, 1] - s[cx, -1] for cx in (-1, 0, 1)}
    jy = ydif[-1] + ydif[0] + ydif[1]
    jz = dsum[-1] + dsum[0] + dsum[1]
    syy = rows[-1] + rows[0] + rows[1]
    szz = total([e[k] for k in e])
    sxy = ydif[1] - ydif[-1]
    sxz = dsum[1] - dsum[-1]
    syz = (d[-1, 1] + d[0, 1] + d[1, 1]) - (d[-1, -1] + d[0, -1] + d[1, -1])
    return rho, jx, jy, jz, sxx, syy, szz, sxy, sxz, syz


def collide(f, mom):
    rho, jx, jy, jz, sxx, syy, szz, sxy, sxz, syz = mom
    inv = 1.0 / rho
    ux, uy, uz = jx * inv, jy * inv, jz * inv
    pxx, pyy, pzz = sxx - jx * ux, syy - jy * uy, szz - jz * uz
    pxy, pxz, pyz = sxy - jx * uy, sxz - jx * uz, syz - jy * uz
    third = (pxx + pyy + pzz) * (1.0 / 3.0)
    qx, qy, qz = 4.5 * (pxx - third), 4.5 * (pyy - third), 4.5 * (pzz - third)
    qxy, qxz, qyz = 9.0 * pxy, 9.0 * pxz, 9.0 * pyz
    base = 1.0 - 1.5 * (ux * ux + uy * uy + uz * uz)
    rest = rho * base - 1.0
    rho3 = 3.0 * rho
    rho45 = 4.5 * rho
    cross = None
    squares = {}
    higher = [None] * 27
    shear = [None] * 27
    for i in range(14):
        c = VELS[i]
        w = WEIGHT[i]
        cls = sum(abs(a) for a in c)
        if i == 13:
            h = f[13] - w * rest
            higher[13] = h
            squares[0] = h * h
            continue
        cu = None
        for a, u in zip(c, (ux, uy, uz)):
            if a:
                cu = (u if a > 0 else -u) if cu is None else (cu + u if a > 0 else cu - u)
        q = None
        for a, v in zip(c, (qx, qy, qz)):
            if a:
                q = v if q is None else q + v
        for a, b, v in ((c[0], c[1], qxy), (c[0], c[2], qxz), (c[1], c[2], qyz)):
            if a * b > 0:
                q = q + v
            elif a * b < 0:
                q = q - v
        even = w * (rest + rho45 * (cu * cu) + q)
        odd = (w * rho3) * cu
        hp = f[i] - even - odd
        hm = f[26 - i] - even + odd
        higher[i], higher[26 - i] = hp, hm
        shear[i] = shear[26 - i] = q
        term = q * (hp + hm)
        cross = term if cross is None else cross + term
        sq = hp * hp + hm * hm
        squares[cls] = sq if cls not in squares else squares[cls] + sq
    norm = squares[0] * (27.0 / 8.0) + squares[1] * 13.5 + squares[2] * 54.0 + squares[3] * 216.0
    gamma = 1.0 / BETA - (2.0 - 1.0 / BETA) * cross / jnp.maximum(norm, FLOOR)
    bg = BETA * gamma
    star = []
    for i in range(27):
        v = f[i] - bg * higher[i]
        if i != 13:
            v = v - (2.0 * BETA * WEIGHT[i]) * shear[i]
        star.append(v)
    return star, (rho, ux, uy, uz)


def pack_pair(m, star_ref, flag_ref, xp_out, yp_out, ym_out):
    source = pl.ds(pl.multiple_of(16 * m + 8, 8), 16)
    target = pl.ds(pl.multiple_of(16 * m, 16), 16)
    lane = lax.broadcasted_iota(jnp.int32, (16, LANES), 1)
    group = (lane // 16).astype(F32).astype(HALO_TYPE)
    slot = (lane % 16).astype(F32).astype(HALO_TYPE)
    star = [star_ref[i, source, :].astype(HALO_TYPE) for i in range(27)]
    flag = None if flag_ref is None else flag_ref[source, :].astype(HALO_TYPE)
    xs = [jnp.zeros((16, LANES), HALO_TYPE) for _ in range(3)]
    for cx in (1, -1):
        edge = 112 if cx > 0 else 0
        for cy in (-1, 0, 1):
            for cz in (-1, 0, 1):
                a, base = x_place(cx, cy, cz)
                xs[a] = jnp.where(group == base // 16, turn(star[pop(cx, cy, cz)], base - edge), xs[a])
        if flag is not None:
            a, base = x_flag_place(cx)
            xs[a] = jnp.where(group == base // 16, turn(flag, base - edge), xs[a])
    for a in range(3):
        xp_out[a, target, :] = xs[a]
    for cy, out in ((1, yp_out), (-1, ym_out)):
        edge = 15 if cy > 0 else 0
        acc = jnp.zeros((16, LANES), HALO_TYPE)
        for cx in (-1, 0, 1):
            for cz in (-1, 0, 1):
                j = y_slot(cx, cz)
                acc = jnp.where(slot == j, turn(star[pop(cx, cy, cz)], 16 * cx + j - edge), acc)
            if flag is not None:
                j = y_flag_slot(cx)
                acc = jnp.where(slot == j, turn(flag, 16 * cx + j - edge), acc)
        out[target, :] = acc


FOLD = 48


def corner_lanes(lane, cx):
    col = 0 if cx > 0 else 112
    slots = [y_slot(cx, cz) for cz in (-1, 0, 1)] + [y_flag_slot(cx)]
    out = lane == col + slots[0]
    for j in slots[1:]:
        out = out | (lane == col + j)
    return out


def corners(yp, ym):
    lane = lax.broadcasted_iota(jnp.int32, yp.shape, 1)
    upper = corner_lanes(lane + 96, -1)
    lines = jnp.where(corner_lanes(lane, 1), yp, jnp.where(upper, turn(yp, -96), turn(ym, 16)))
    lane = lane[:FOLD]
    out = lines[:FOLD]
    for k in range(1, HALO_ROWS // FOLD):
        out = jnp.where(lane // 32 == k, turn(lines[k * FOLD : (k + 1) * FOLD], 32 * k), out)
    return out


def initial_kernel(perturb_hbm, density_hbm, velocity_hbm, excitation_hbm, solid_hbm, f_out, lo_out, hi_out, s_out,
                   perturb, density, velocity, excitation, solid, chunk_sem, sem):
    small = [
        pltpu.make_async_copy(src, dst, sem.at[k])
        for k, (src, dst) in enumerate(((density_hbm, density), (velocity_hbm, velocity),
                                        (excitation_hbm, excitation), (solid_hbm, solid)))
    ]
    for copy in small:
        copy.start()
    chunks = [
        pltpu.make_async_copy(perturb_hbm.at[pl.ds(3 * k, 3)], perturb.at[pl.ds(3 * k, 3)], chunk_sem.at[k])
        for k in range(9)
    ]
    for copy in chunks:
        copy.start()
    for copy in small:
        copy.wait()
    rho = density[...]
    ux, uy, uz = velocity[0], velocity[1], velocity[2]
    amplitude = excitation[...]
    base = 1.0 - 1.5 * (ux * ux + uy * uy + uz * uz)

    def put(i, v, out):
        out[FIRST : FIRST + 128, :] = v
        lo_out[4 * i : 4 * i + 4, :] = v[0:4, :]
        hi_out[4 * i : 4 * i + 4, :] = v[124:128, :]

    put(27, solid[...].astype(F32).T, s_out)
    for i in range(27):
        c = VELS[i]
        shape = base
        cu = None
        for a, u in zip(c, (ux, uy, uz)):
            if a:
                cu = (u if a > 0 else -u) if cu is None else (cu + u if a > 0 else cu - u)
        if cu is not None:
            shape = shape + 3.0 * cu + 4.5 * (cu * cu)
        if i % 3 == 0:
            chunks[i // 3].wait()
        v = WEIGHT[i] * (rho * shape * (1.0 + amplitude * perturb[i]) - 1.0)
        put(i, v.T, f_out.at[i])


def first_kernel(f_in, s_in, lo, hi, unused, star_out, s_out, xp_out, yp_out, ym_out, xc_out, edge):
    for i in range(28):
        below = lo[4 * i : 4 * i + 4, :]
        above = hi[4 * i : 4 * i + 4, :]
        edge[i, 0:4, :] = below
        edge[i, 4:8, :] = below
        edge[i, 8:12, :] = above
        edge[i, 12:16, :] = above

    def emit(t, load):
        f = [load(i) for i in range(27)]
        star, _ = collide(f, moments(f))
        at = pl.ds(pl.multiple_of(8 * t, 8), 8)
        for i in range(27):
            star_out[i, at, :] = star[i]
        s_out[at, :] = load(27)

    def pack_at(m):
        pack_pair(m, star_out, s_out, xp_out, yp_out, ym_out)

    def outer(k, carry):
        at = pl.ds(pl.multiple_of(8 * k, 8), 8)
        emit(1 + 17 * k, lambda i: edge[i, at, :])
        return carry

    def inner(k, carry):
        pack_at(jnp.maximum(k - 1, 0))
        for t in (2 * k + 2, 2 * k + 3):
            at = pl.ds(pl.multiple_of(8 * t, 8), 8)
            emit(t, lambda i: s_in[at, :] if i == 27 else f_in[i, at, :])
        return carry

    lax.fori_loop(0, 2, outer, 0)
    lax.fori_loop(0, 8, inner, 0)
    pack_at(7)
    pack_at(8)
    xc_out[...] = corners(yp_out[...].astype(F32), ym_out[...].astype(F32)).astype(xc_out.dtype)


def patch_kernel(low, high, yp_in, ym_in, yp_out, ym_out):
    lane = lax.broadcasted_iota(jnp.int32, (FOLD, LANES), 1)
    got = {1: low[...].astype(F32), -1: high[...].astype(F32)}
    for shift, source, out in (({1: 0, -1: 96}, yp_in, yp_out), ({1: -16, -1: 112}, ym_in, ym_out)):
        for k in range(HALO_ROWS // FOLD):
            acc = source[k * FOLD : (k + 1) * FOLD, :].astype(F32)
            for cx in (1, -1):
                acc = jnp.where(corner_lanes(lane, cx), turn(got[cx], shift[cx] - 32 * k), acc)
            out[k * FOLD : (k + 1) * FOLD, :] = acc.astype(out.dtype)


def step_kernel(first, last, *refs):
    refs = list(refs)
    star_in, s_in, xh, yph, ymh, _ = refs[:6]
    refs = refs[6:]
    if last:
        mom_out = refs.pop(0)
        star_out = None
    else:
        mom_out, star_out, xp_out, yp_out, ym_out, xc_out = refs[:6]
        refs = refs[6:]
    if first:
        wall_ref = refs.pop(0)
    else:
        wall_ref = s_in
    xs, ys = refs[:2]
    lane = lane_iota()
    slot = lane % 16
    halo = pl.ds(8, HALO_ROWS)

    for a in range(3):
        xs[a, halo, :] = xh[a].astype(F32)
    ys[0, halo, :] = yph[...].astype(F32)
    ys[1, halo, :] = ymh[...].astype(F32)
    edge_rows = (pl.ds(0, 8), pl.ds(ROWS - 8, 8))
    for at in edge_rows:
        for a in range(3):
            xs[a, at, :] = jnp.zeros((8, LANES), F32)
        for a in range(2):
            ys[a, at, :] = jnp.zeros((8, LANES), F32)
        if first:
            for k in range(9):
                wall_ref[k, at, :] = jnp.zeros((8, LANES), F32)

    def gather(v, cx, cy, x_at, x_load, y_slot_of, y_load):
        v = turn(v, 16 * cx + cy)
        if cx:
            a, base = x_at
            if cx > 0:
                v = jnp.where(lane < 16, turn(x_load(a), cy - base), v)
            else:
                v = jnp.where(lane >= 112, turn(x_load(a), 112 - base + cy), v)
        if cy > 0:
            v = jnp.where(slot == 0, turn(y_load(0), -y_slot_of), v)
        elif cy < 0:
            v = jnp.where(slot == 15, turn(y_load(1), 15 - y_slot_of), v)
        return v

    if first:
        def walls(k, carry):
            at = pl.ds(pl.multiple_of(8 * k + 8, 8), 8)
            flag = s_in[at, :]
            for cx in (-1, 0, 1):
                for cy in (-1, 0, 1):
                    wall_ref[(cx + 1) * 3 + cy + 1, at, :] = gather(
                        flag, cx, cy, x_flag_place(cx), lambda a: xs[a, at, :],
                        y_flag_slot(cx), lambda a: ys[a, at, :])
            return carry

        lax.fori_loop(0, TILES, walls, 0, unroll=6)

    def gather_tile(t, buf):
        here = pl.ds(pl.multiple_of(8 * t, 8), 8)
        for i in range(27):
            cx, cy, cz = VELS[i]
            at = here if cz == 0 else pl.ds(8 * t - cz, 8)
            v = star_in[i, at, :]
            if i != 13:
                v = gather(v, cx, cy, x_place(cx, cy, cz), lambda a: xs[a, at, :],
                           y_slot(cx, cz), lambda a: ys[a, at, :])
                wall = wall_ref[(cx + 1) * 3 + cy + 1, at, :]
                v = jnp.where(wall > 0.5, star_in[26 - i, here, :], v)
            buf[i] = v

    def collide_tile(t, buf):
        f = [buf[i] for i in range(27)]
        mom = moments(f)
        if last:
            inv = 1.0 / mom[0]
            macro = mom[0], mom[1] * inv, mom[2] * inv, mom[3] * inv
        else:
            star, macro = collide(f, mom)
            here = pl.ds(pl.multiple_of(8 * t, 8), 8)
            for i in range(27):
                star_out[i, here, :] = star[i]
        row = pl.ds(pl.multiple_of(8 * t - 8, 8), 8)
        for a, v in enumerate(macro):
            mom_out[a, row, :] = v

    even, odd = refs[2:4]

    def pack_at(m):
        if not last:
            pack_pair(m, star_out, None, xp_out, yp_out, ym_out)

    def body(m, carry):
        collide_tile(2 * m + 1, even)
        gather_tile(2 * m + 2, odd)
        pack_at(jnp.maximum(m - 1, 0))
        collide_tile(2 * m + 2, odd)
        gather_tile(jnp.minimum(2 * m + 3, TILES), even)
        return carry

    gather_tile(1, even)
    lax.fori_loop(0, TILES // 2, body, 0)
    pack_at(TILES // 2 - 1)
    if not last:
        xc_out[...] = corners(yp_out[...].astype(F32), ym_out[...].astype(F32)).astype(xc_out.dtype)


def prepare_kernel(capacity, owner_row, owner_col, cell, placing_out, lane_out, row_out):
    slots = owner_row.shape[1]
    q = lax.broadcasted_iota(jnp.int32, (slots, slots), 0)
    p = lax.broadcasted_iota(jnp.int32, (slots, slots), 1)
    same = (owner_row[...] == owner_col[...]) & (q < p)
    rank = jnp.sum(same.astype(F32), axis=0, keepdims=True).astype(jnp.int32)
    column = owner_row[...] * capacity + rank
    rows = placing_out.shape[0]
    placing_out[...] = (lax.broadcasted_iota(jnp.int32, (rows, slots), 0) == column).astype(F32).astype(jnp.bfloat16)
    k = lax.broadcasted_iota(jnp.int32, (LANES, slots), 0)
    lane_out[...] = (k == cell[...] // 128).astype(F32).astype(jnp.bfloat16)
    row_out[...] = (k == cell[...] % 128).astype(F32)


def split3(v):
    hi = v.astype(jnp.bfloat16)
    left = v - hi.astype(F32)
    mid = left.astype(jnp.bfloat16)
    low = (left - mid.astype(F32)).astype(jnp.bfloat16)
    return hi, mid, low


def sample_rows(upper, mom, lane_hot, row_hot, area, placing):
    fields = []
    hot = row_hot[...]
    lanes = lane_hot[...]
    for a in range(4):
        picked = None
        for part in split3(mom[a, 8 : 8 + 128, :]):
            term = jnp.dot(part, lanes, preferred_element_type=F32)
            picked = term if picked is None else picked + term
        fields.append(jnp.sum(picked * hot, axis=0, keepdims=True))
    rho, u = fields[0], fields[1:]
    pressure = (rho - 1.0) / 3.0
    normal = [area[j : j + 1, :] for j in range(3)]
    flow = u[0] * normal[0] + u[1] * normal[1] + u[2] * normal[2]
    rows = [rho * flow] + [pressure * normal[j] + rho * u[j] * flow for j in range(3)]
    blank = [jnp.zeros_like(rho)] * 4
    stacked = jnp.concatenate(blank + rows if upper else rows + blank, axis=0).astype(jnp.bfloat16)
    return lax.dot_general(stacked, placing[...], (((1,), (1,)), ((), ())), preferred_element_type=F32)


def sample_kernel(upper, *refs):
    refs[-1][...] = sample_rows(upper, *refs[:-1])


def scatter_kernel(groups, capacity, mom, lane_hot, row_hot, area, placing, part0, part1, part2, out):
    last = sample_rows(1, mom, lane_hot, row_hot, area, placing)
    pairs = [part0[...] + part1[...], part2[...] + last]
    lane = lane_iota()
    for g in range(groups):
        start = g * capacity
        tile = slice(start // LANES * LANES, start // LANES * LANES + LANES)
        low = turn(pairs[0][:, tile], -start)
        high = turn(pairs[1][:, tile], 64 - start)
        value = jnp.where(lane < 64, low, high)
        out[g] = value


def fetch_kernel(weights_hbm, unused, out, sem):
    copy = pltpu.make_async_copy(weights_hbm.at[pl.ds(0, out.shape[0])], out, sem.at[0])
    copy.start()
    copy.wait()


def window_kernel(solid_hbm, mom, unused, density_out, velocity_out, solid, sem):
    copy = pltpu.make_async_copy(solid_hbm, solid, sem.at[0])
    copy.start()
    copy.wait()
    wall = solid[...] != 0
    density_out[...] = jnp.where(wall, 1.0, mom[0, 8:136, :].T)
    for a in range(3):
        velocity_out[a] = jnp.where(wall, 0.0, mom[a + 1, 8:136, :].T)


def observe_kernel(groups, capacity, ptile, weights_hbm, near, offset, rec, out, rest, sem):
    ahead = near.shape[0]
    copy = pltpu.make_async_copy(weights_hbm.at[pl.ds(ahead, 4 - ahead)], rest, sem.at[0])
    copy.start()
    obs = rest.shape[2]
    part = obs // 2
    tiles = offset.shape[0]
    rows = groups * capacity
    halves = []
    lane = lane_iota()
    per = LANES // capacity
    for half in range(2):
        pieces = []
        for start in range(0, groups, per):
            acc = jnp.zeros((8, LANES), F32)
            for g in range(start, start + per):
                moved = turn(rec[g], (g - start) * capacity - 64 * half)
                acc = jnp.where(lane // capacity == g - start, moved, acc)
            pieces.append(acc)
        halves.append(jnp.concatenate(pieces, axis=1))
    keep = lax.broadcasted_iota(jnp.int32, (tiles, rows), 1) // ptile == lax.broadcasted_iota(jnp.int32, (tiles, rows), 0)
    lefts = []
    for k in range(4):
        left = [
            jnp.where(keep, jnp.broadcast_to(halves[s // 2][4 * (s % 2) + k : 4 * (s % 2) + k + 1, :], (tiles, rows)), 0.0)
            for s in range(STEPS)
        ]
        lefts.append(jnp.concatenate(left, axis=0).astype(jnp.bfloat16))
    devices = out.shape[0]
    count = obs // devices
    obs_tile = obs // offset.shape[1]
    for h in range(2):
        acc = None
        for k in range(4):
            if k == ahead and h == 0:
                copy.wait()
            cols = slice(h * part, (h + 1) * part)
            right = near[k, :, cols] if k < ahead else rest[k - ahead, :, cols]
            term = jnp.dot(lefts[k], right, preferred_element_type=F32)
            acc = term if acc is None else acc + term
        peak = jnp.max(jnp.max(jnp.abs(acc), axis=1, keepdims=True), axis=0, keepdims=True)
        power = jnp.broadcast_to(jnp.ceil(jnp.log2(jnp.maximum(peak, 1e-30))), (tiles, LANES))
        down = jnp.exp2(TOP - power)
        for d in range(h * devices // 2, (h + 1) * devices // 2):
            start = d * count
            here = start - h * part
            piece = jnp.zeros((tiles, LANES), F32)
            for s in range(STEPS):
                block = acc[tiles * s : tiles * (s + 1), here // LANES * LANES : here // LANES * LANES + LANES]
                moved = turn(block, s * count - start % LANES)
                piece = jnp.where(lane // count == s, moved, piece)
            out[d, 0:tiles, :] = piece * down
            o = start // obs_tile
            out[d, tiles : 2 * tiles, :] = jnp.where(lane < 64, jnp.broadcast_to(offset[:, o : o + 1], (tiles, LANES)), power)


def signal_kernel(got, out):
    devices, twice = got.shape[0], got.shape[1]
    tiles = twice // 2
    count = out.shape[0]
    shape = (devices * tiles, LANES)
    notes = got[:, tiles:twice, :].reshape(shape)
    start = jnp.broadcast_to(notes[:, 0:1], shape)
    values = got[:, 0:tiles, :].reshape(shape) * jnp.exp2(jnp.broadcast_to(notes[:, 64:65], shape) - TOP)
    bins = lax.broadcasted_iota(jnp.int32, (devices * tiles, NB), 1).astype(F32)
    hot = (start == bins).astype(F32).astype(jnp.bfloat16)
    acc = None
    for part in split3(values):
        term = lax.dot_general(part, hot, (((0,), (0,)), ((), ())), preferred_element_type=F32)
        acc = term if acc is None else acc + term
    total = None
    for s in range(STEPS):
        moved = turn(acc[s * count : (s + 1) * count, :], s)
        total = moved if total is None else total + moved
    out[...] = total


def call(kernel, outs, *args, scratch=(), flops=1000000, limit=24, far=()):
    args = [pltpu.with_memory_space_constraint(a, pltpu.HBM) if k in far else a for k, a in enumerate(args)]
    return pl.pallas_call(
        kernel,
        out_shape=outs,
        in_specs=[pl.BlockSpec(memory_space=pltpu.HBM if k in far else pltpu.VMEM) for k in range(len(args))],
        out_specs=jax.tree.map(lambda _: pl.BlockSpec(memory_space=pltpu.VMEM), outs),
        scratch_shapes=list(scratch),
        compiler_params=pltpu.CompilerParams(vmem_limit_bytes=limit << 20),
        cost_estimate=pl.CostEstimate(
            flops=flops, transcendentals=0,
            bytes_accessed=sum(a.size * a.dtype.itemsize for a in args)),
    )(*args)


def ring(axis, shift):
    count = lax.axis_size(axis)
    return [(i, (i + shift) % count) for i in range(count)]


def shift(value, axis, by):
    return lax.ppermute(value, axis, ring(axis, by))


def exchange(xp, yp, ym, xc):
    if lax.axis_size("gx") == 2:
        low = high = shift(xc, "gx", 1)
        xh = shift(xp, "gx", 1)
    else:
        low = shift(xc, "gx", 1)
        high = shift(xc, "gx", -1)
        up = shift(jnp.stack([xp[0], xp[2]]), "gx", 1)
        down = shift(jnp.stack([xp[1], xp[2]]), "gx", -1)
        xh = jnp.stack([up[0], down[0], jnp.where(jnp.arange(LANES) < 64, up[1], down[1])])
    face = jax.ShapeDtypeStruct((HALO_ROWS, LANES), HALO_TYPE)
    yp, ym = call(patch_kernel, (face, face), low, high, yp, ym)
    return xh, shift(yp, "gy", 1), shift(ym, "gy", -1)


def shards(perturb, density, velocity, excitation, solid_flag, panel_cell, panel_owner, panel_area, weights, bin_offset):
    bx, by, bz = density.shape
    assert bx * by == LANES and bz == LANES and by == 16
    flat = (LANES, LANES)
    solid = solid_flag.reshape(flat)
    block = jax.ShapeDtypeStruct((27, ROWS, LANES), F32)
    one = jax.ShapeDtypeStruct((ROWS, LANES), F32)
    rim = jax.ShapeDtypeStruct((28 * 4, LANES), F32)
    x_face = jax.ShapeDtypeStruct((3, HALO_ROWS, LANES), HALO_TYPE)
    y_face = jax.ShapeDtypeStruct((HALO_ROWS, LANES), HALO_TYPE)
    x_edge = jax.ShapeDtypeStruct((FOLD, LANES), HALO_TYPE)

    f0, low_rim, high_rim, flags = call(
        initial_kernel, (block, rim, rim, one),
        perturb.reshape((27,) + flat), density.reshape(flat), velocity.reshape((3,) + flat),
        excitation.reshape(flat), solid,
        far=range(5),
        scratch=(pltpu.VMEM((27,) + flat, F32), pltpu.VMEM(flat, F32), pltpu.VMEM((3,) + flat, F32), pltpu.VMEM(flat, F32),
                 pltpu.VMEM(flat, jnp.int32), pltpu.SemaphoreType.DMA((9,)), pltpu.SemaphoreType.DMA((4,))))
    below = lax.ppermute(high_rim, "gz", ring("gz", 1))
    above = lax.ppermute(low_rim, "gz", ring("gz", -1))

    group_count = lax.axis_size(("gx", "gy"))
    slots = panel_owner.shape[0]
    row_count = 2 * slots
    capacity = row_count // group_count
    placing, lane_hot, row_hot = call(
        functools.partial(prepare_kernel, capacity),
        (jax.ShapeDtypeStruct((row_count, slots), jnp.bfloat16),
         jax.ShapeDtypeStruct((LANES, slots), jnp.bfloat16),
         jax.ShapeDtypeStruct((LANES, slots), F32)),
        panel_owner.reshape(1, slots), panel_owner.reshape(slots, 1), panel_cell.reshape(1, slots))

    star, walls, xp, yp, ym, xc = call(
        first_kernel, (block, one, x_face, y_face, y_face, x_edge), f0, flags, below, above, placing,
        scratch=(pltpu.VMEM((28, 16, LANES), F32),))

    mom_shape = jax.ShapeDtypeStruct((4, HALO_ROWS, LANES), F32)
    routed = []
    for s in range(STEPS):
        first, last = s == 0, s == STEPS - 1
        xh, yph, ymh = exchange(xp, yp, ym, xc)
        outs = [mom_shape]
        if not last:
            outs += [block, x_face, y_face, y_face, x_edge]
        if first:
            outs += [jax.ShapeDtypeStruct((9, ROWS, LANES), F32)]
        scratch = [pltpu.VMEM((3, ROWS, LANES), F32), pltpu.VMEM((2, ROWS, LANES), F32)]
        scratch += [pltpu.VMEM((27, 8, LANES), F32)] * 2
        res = call(functools.partial(step_kernel, first, last), tuple(outs), star, walls, xh, yph, ymh,
                   routed[-1] if routed else placing, scratch=scratch)
        mom = res[0]
        if not last:
            star, xp, yp, ym, xc = res[1:6]
        if first:
            walls = res[6]
        if not last:
            routed.append(call(functools.partial(sample_kernel, s % 2), jax.ShapeDtypeStruct((8, row_count), F32),
                               mom, lane_hot, row_hot, panel_area, placing))

    send = functools.partial(scatter_kernel, group_count, capacity)
    samples = (mom, lane_hot, row_hot, panel_area, placing, *routed)

    def fetch(count, after):
        return call(fetch_kernel,
                    jax.ShapeDtypeStruct((count,) + weights.shape[1:], weights.dtype), weights, after, far=(0,),
                    scratch=(pltpu.SemaphoreType.DMA((1,)),))

    sent = call(send, jax.ShapeDtypeStruct((group_count, 8, LANES), F32), *samples)
    received = lax.all_to_all(sent, ("gx", "gy"), split_axis=0, concat_axis=0, tiled=True)
    near = fetch(3, sent)

    tiles, obs_tiles = bin_offset.shape
    devices = lax.axis_size(("gx", "gy", "gz"))
    obs = weights.shape[2]
    count = obs // devices
    assert obs // obs_tiles % count == 0 and tiles % 8 == 0 and STEPS * count <= LANES and capacity <= 64
    out_shape = (devices, 2 * tiles, LANES)
    observed = pl.pallas_call(
        functools.partial(observe_kernel, group_count, capacity, row_count // tiles),
        out_shape=jax.ShapeDtypeStruct(out_shape, F32),
        in_specs=[pl.BlockSpec(memory_space=pltpu.HBM)] + [pl.BlockSpec(memory_space=pltpu.VMEM)] * 3,
        out_specs=pl.BlockSpec(memory_space=pltpu.VMEM),
        scratch_shapes=[pltpu.VMEM((4 - near.shape[0],) + weights.shape[1:], weights.dtype),
                        pltpu.SemaphoreType.DMA((1,))],
        compiler_params=pltpu.CompilerParams(vmem_limit_bytes=24 << 20),
    )(pltpu.with_memory_space_constraint(weights, pltpu.HBM), near, bin_offset.astype(F32), received)
    final_density, final_velocity = call(
        window_kernel,
        (jax.ShapeDtypeStruct(flat, F32), jax.ShapeDtypeStruct((3,) + flat, F32)),
        solid, mom, sent, far=(0,), scratch=(pltpu.VMEM(flat, jnp.int32), pltpu.SemaphoreType.DMA((1,))))
    got = lax.all_to_all(observed.astype(jnp.float16), ("gx", "gy", "gz"), split_axis=0, concat_axis=0, tiled=True)
    signal = call(signal_kernel, jax.ShapeDtypeStruct((count, NB), F32), got.astype(F32))
    return final_density.reshape(density.shape), final_velocity.reshape(velocity.shape), signal


def solution(mesh):
    cells = P("gx", "gy", "gz")
    vectors = P(None, "gx", "gy", "gz")
    every = ("gx", "gy", "gz")
    placed = (vectors, cells, vectors, cells, cells, P(every), P(every), P(None, every), P(None, every, None), P(every, None))
    return jax.shard_map(
        shards, mesh=mesh, in_specs=placed, out_specs=(cells, vectors, P(every, None)), check_vma=False)
```

```python
import functools
import jax
import jax.numpy as jnp
from jax import lax
from jax.experimental import pallas as pl
from jax.experimental.pallas import tpu as pltpu
from jax.sharding import PartitionSpec as P


STEPS = 4
NB = 128
BETA = 0.99
FLOOR = 1e-06
LANES = 128
ROWS = 160
FIRST = 16
TILES = 18
HALO_ROWS = 8 * TILES
HALO_TYPE = jnp.bfloat16
F32 = jnp.float32
TOP = 14.0


VELS = [(i // 9 - 1, (i // 3) % 3 - 1, i % 3 - 1) for i in range(27)]
WEIGHT = [float([8 / 27, 2 / 27, 1 / 54, 1 / 216][sum(abs(a) for a in c)]) for c in VELS]


def pop(cx, cy, cz):
    return (cx + 1) * 9 + (cy + 1) * 3 + cz + 1


def x_place(cx, cy, cz):
    j = (cy + 1) * 3 + cz + 1
    if j < 8:
        return (0 if cx > 0 else 1), 16 * j
    return 2, (0 if cx > 0 else 64)


def x_flag_place(cx):
    return 2, (16 if cx > 0 else 80)


def y_slot(cx, cz):
    return (cx + 1) * 3 + cz + 1


def y_flag_slot(cx):
    return 9 + cx + 1


def lane_iota():
    return lax.broadcasted_iota(jnp.int32, (8, LANES), 1)


def turn(v, shift):
    shift %= LANES
    return v if shift == 0 else pltpu.roll(v, shift, 1)


def moments(f):
    def total(vals):
        vals = list(vals)
        while len(vals) > 1:
            vals = [a + b for a, b in zip(vals[::2], vals[1::2])] + ([vals[-1]] if len(vals) % 2 else [])
        return vals[0]

    s = {}
    d = {}
    e = {}
    for cx in (-1, 0, 1):
        for cy in (-1, 0, 1):
            lo, mid, hi = f[pop(cx, cy, -1)], f[pop(cx, cy, 0)], f[pop(cx, cy, 1)]
            e[cx, cy] = lo + hi
            d[cx, cy] = hi - lo
            s[cx, cy] = mid + e[cx, cy]
    rows = {cx: s[cx, -1] + s[cx, 1] for cx in (-1, 0, 1)}
    full = {cx: rows[cx] + s[cx, 0] for cx in (-1, 0, 1)}
    dsum = {cx: d[cx, -1] + d[cx, 0] + d[cx, 1] for cx in (-1, 0, 1)}
    sxx = full[-1] + full[1]
    rho = 1.0 + (sxx + full[0])
    jx = full[1] - full[-1]
    ydif = {cx: s[cx, 1] - s[cx, -1] for cx in (-1, 0, 1)}
    jy = ydif[-1] + ydif[0] + ydif[1]
    jz = dsum[-1] + dsum[0] + dsum[1]
    syy = rows[-1] + rows[0] + rows[1]
    szz = total([e[k] for k in e])
    sxy = ydif[1] - ydif[-1]
    sxz = dsum[1] - dsum[-1]
    syz = (d[-1, 1] + d[0, 1] + d[1, 1]) - (d[-1, -1] + d[0, -1] + d[1, -1])
    return rho, jx, jy, jz, sxx, syy, szz, sxy, sxz, syz


def collide(f, mom):
    rho, jx, jy, jz, sxx, syy, szz, sxy, sxz, syz = mom
    inv = 1.0 / rho
    ux, uy, uz = jx * inv, jy * inv, jz * inv
    pxx, pyy, pzz = sxx - jx * ux, syy - jy * uy, szz - jz * uz
    pxy, pxz, pyz = sxy - jx * uy, sxz - jx * uz, syz - jy * uz
    third = (pxx + pyy + pzz) * (1.0 / 3.0)
    qx, qy, qz = 4.5 * (pxx - third), 4.5 * (pyy - third), 4.5 * (pzz - third)
    qxy, qxz, qyz = 9.0 * pxy, 9.0 * pxz, 9.0 * pyz
    base = 1.0 - 1.5 * (ux * ux + uy * uy + uz * uz)
    rest = rho * base - 1.0
    rho3 = 3.0 * rho
    rho45 = 4.5 * rho
    cross = None
    squares = {}
    higher = [None] * 27
    shear = [None] * 27
    for i in range(14):
        c = VELS[i]
        w = WEIGHT[i]
        cls = sum(abs(a) for a in c)
        if i == 13:
            h = f[13] - w * rest
            higher[13] = h
            squares[0] = h * h
            continue
        cu = None
        for a, u in zip(c, (ux, uy, uz)):
            if a:
                cu = (u if a > 0 else -u) if cu is None else (cu + u if a > 0 else cu - u)
        q = None
        for a, v in zip(c, (qx, qy, qz)):
            if a:
                q = v if q is None else q + v
        for a, b, v in ((c[0], c[1], qxy), (c[0], c[2], qxz), (c[1], c[2], qyz)):
            if a * b > 0:
                q = q + v
            elif a * b < 0:
                q = q - v
        even = w * (rest + rho45 * (cu * cu) + q)
        odd = (w * rho3) * cu
        hp = f[i] - even - odd
        hm = f[26 - i] - even + odd
        higher[i], higher[26 - i] = hp, hm
        shear[i] = shear[26 - i] = q
        term = q * (hp + hm)
        cross = term if cross is None else cross + term
        sq = hp * hp + hm * hm
        squares[cls] = sq if cls not in squares else squares[cls] + sq
    norm = squares[0] * (27.0 / 8.0) + squares[1] * 13.5 + squares[2] * 54.0 + squares[3] * 216.0
    gamma = 1.0 / BETA - (2.0 - 1.0 / BETA) * cross / jnp.maximum(norm, FLOOR)
    bg = BETA * gamma
    star = []
    for i in range(27):
        v = f[i] - bg * higher[i]
        if i != 13:
            v = v - (2.0 * BETA * WEIGHT[i]) * shear[i]
        star.append(v)
    return star, (rho, ux, uy, uz)


def pack_pair(m, star_ref, flag_ref, xp_out, yp_out, ym_out):
    source = pl.ds(pl.multiple_of(16 * m + 8, 8), 16)
    target = pl.ds(pl.multiple_of(16 * m, 16), 16)
    lane = lax.broadcasted_iota(jnp.int32, (16, LANES), 1)
    group = (lane // 16).astype(F32).astype(HALO_TYPE)
    slot = (lane % 16).astype(F32).astype(HALO_TYPE)
    star = [star_ref[i, source, :].astype(HALO_TYPE) for i in range(27)]
    flag = None if flag_ref is None else flag_ref[source, :].astype(HALO_TYPE)
    xs = [jnp.zeros((16, LANES), HALO_TYPE) for _ in range(3)]
    for cx in (1, -1):
        edge = 112 if cx > 0 else 0
        for cy in (-1, 0, 1):
            for cz in (-1, 0, 1):
                a, base = x_place(cx, cy, cz)
                xs[a] = jnp.where(group == base // 16, turn(star[pop(cx, cy, cz)], base - edge), xs[a])
        if flag is not None:
            a, base = x_flag_place(cx)
            xs[a] = jnp.where(group == base // 16, turn(flag, base - edge), xs[a])
    for a in range(3):
        xp_out[a, target, :] = xs[a]
    for cy, out in ((1, yp_out), (-1, ym_out)):
        edge = 15 if cy > 0 else 0
        acc = jnp.zeros((16, LANES), HALO_TYPE)
        for cx in (-1, 0, 1):
            for cz in (-1, 0, 1):
                j = y_slot(cx, cz)
                acc = jnp.where(slot == j, turn(star[pop(cx, cy, cz)], 16 * cx + j - edge), acc)
            if flag is not None:
                j = y_flag_slot(cx)
                acc = jnp.where(slot == j, turn(flag, 16 * cx + j - edge), acc)
        out[target, :] = acc


FOLD = 48


def corner_lanes(lane, cx):
    col = 0 if cx > 0 else 112
    slots = [y_slot(cx, cz) for cz in (-1, 0, 1)] + [y_flag_slot(cx)]
    out = lane == col + slots[0]
    for j in slots[1:]:
        out = out | (lane == col + j)
    return out


def corners(yp, ym):
    lane = lax.broadcasted_iota(jnp.int32, yp.shape, 1)
    upper = corner_lanes(lane + 96, -1)
    lines = jnp.where(corner_lanes(lane, 1), yp, jnp.where(upper, turn(yp, -96), turn(ym, 16)))
    lane = lane[:FOLD]
    out = lines[:FOLD]
    for k in range(1, HALO_ROWS // FOLD):
        out = jnp.where(lane // 32 == k, turn(lines[k * FOLD : (k + 1) * FOLD], 32 * k), out)
    return out


def initial_kernel(perturb_hbm, density_hbm, velocity_hbm, excitation_hbm, solid_hbm, f_out, lo_out, hi_out, s_out,
                   perturb, density, velocity, excitation, solid, lo_tmp, hi_tmp, chunk_sem, sem):
    small = [
        pltpu.make_async_copy(src, dst, sem.at[k])
        for k, (src, dst) in enumerate(((density_hbm, density), (velocity_hbm, velocity),
                                        (excitation_hbm, excitation), (solid_hbm, solid)))
    ]
    for copy in small:
        copy.start()
    chunks = [
        pltpu.make_async_copy(perturb_hbm.at[pl.ds(3 * k, 3)], perturb.at[pl.ds(3 * k, 3)], chunk_sem.at[k])
        for k in range(9)
    ]
    for copy in chunks:
        copy.start()
    for copy in small:
        copy.wait()
    rho = density[...]
    ux, uy, uz = velocity[0], velocity[1], velocity[2]
    amplitude = excitation[...]
    base = 1.0 - 1.5 * (ux * ux + uy * uy + uz * uz)

    def put(i, v, out):
        out[FIRST : FIRST + 128, :] = v
        lo_tmp[4 * i : 4 * i + 4, :] = v[0:4, :]
        hi_tmp[4 * i : 4 * i + 4, :] = v[124:128, :]

    put(27, solid[...].astype(F32).T, s_out)
    for i in range(27):
        c = VELS[i]
        shape = base
        cu = None
        for a, u in zip(c, (ux, uy, uz)):
            if a:
                cu = (u if a > 0 else -u) if cu is None else (cu + u if a > 0 else cu - u)
        if cu is not None:
            shape = shape + 3.0 * cu + 4.5 * (cu * cu)
        if i % 3 == 0:
            chunks[i // 3].wait()
        v = WEIGHT[i] * (rho * shape * (1.0 + amplitude * perturb[i]) - 1.0)
        put(i, v.T, f_out.at[i])
    lo_out[...] = lo_tmp[...].astype(lo_out.dtype)
    hi_out[...] = hi_tmp[...].astype(hi_out.dtype)


def first_kernel(f_in, s_in, lo, hi, unused, star_out, s_out, xp_out, yp_out, ym_out, xc_out, edge, lo_tmp, hi_tmp):
    lo_tmp[...] = lo[...].astype(F32)
    hi_tmp[...] = hi[...].astype(F32)
    for i in range(28):
        below = lo_tmp[4 * i : 4 * i + 4, :]
        above = hi_tmp[4 * i : 4 * i + 4, :]
        edge[i, 0:4, :] = below
        edge[i, 4:8, :] = below
        edge[i, 8:12, :] = above
        edge[i, 12:16, :] = above

    def emit(t, load):
        f = [load(i) for i in range(27)]
        star, _ = collide(f, moments(f))
        at = pl.ds(pl.multiple_of(8 * t, 8), 8)
        for i in range(27):
            star_out[i, at, :] = star[i]
        s_out[at, :] = load(27)

    def pack_at(m):
        pack_pair(m, star_out, s_out, xp_out, yp_out, ym_out)

    def outer(k, carry):
        at = pl.ds(pl.multiple_of(8 * k, 8), 8)
        emit(1 + 17 * k, lambda i: edge[i, at, :])
        return carry

    def inner(k, carry):
        pack_at(jnp.maximum(k - 1, 0))
        for t in (2 * k + 2, 2 * k + 3):
            at = pl.ds(pl.multiple_of(8 * t, 8), 8)
            emit(t, lambda i: s_in[at, :] if i == 27 else f_in[i, at, :])
        return carry

    lax.fori_loop(0, 2, outer, 0)
    lax.fori_loop(0, 8, inner, 0)
    pack_at(7)
    pack_at(8)
    xc_out[...] = corners(yp_out[...].astype(F32), ym_out[...].astype(F32)).astype(xc_out.dtype)


def patch_kernel(low, high, yp_in, ym_in, yp_out, ym_out):
    lane = lax.broadcasted_iota(jnp.int32, (FOLD, LANES), 1)
    got = {1: low[...].astype(F32), -1: high[...].astype(F32)}
    for shift, source, out in (({1: 0, -1: 96}, yp_in, yp_out), ({1: -16, -1: 112}, ym_in, ym_out)):
        for k in range(HALO_ROWS // FOLD):
            acc = source[k * FOLD : (k + 1) * FOLD, :].astype(F32)
            for cx in (1, -1):
                acc = jnp.where(corner_lanes(lane, cx), turn(got[cx], shift[cx] - 32 * k), acc)
            out[k * FOLD : (k + 1) * FOLD, :] = acc.astype(out.dtype)


def step_kernel(first, last, *refs):
    refs = list(refs)
    star_in, s_in, xh, yph, ymh, _ = refs[:6]
    refs = refs[6:]
    if last:
        mom_out = refs.pop(0)
        star_out = None
    else:
        mom_out, star_out, xp_out, yp_out, ym_out, xc_out = refs[:6]
        refs = refs[6:]
    if first:
        wall_ref = refs.pop(0)
    else:
        wall_ref = s_in
    xs, ys = refs[:2]
    lane = lane_iota()
    slot = lane % 16
    halo = pl.ds(8, HALO_ROWS)

    for a in range(3):
        xs[a, halo, :] = xh[a].astype(F32)
    ys[0, halo, :] = yph[...].astype(F32)
    ys[1, halo, :] = ymh[...].astype(F32)
    edge_rows = (pl.ds(0, 8), pl.ds(ROWS - 8, 8))
    for at in edge_rows:
        for a in range(3):
            xs[a, at, :] = jnp.zeros((8, LANES), F32)
        for a in range(2):
            ys[a, at, :] = jnp.zeros((8, LANES), F32)
        if first:
            for k in range(9):
                wall_ref[k, at, :] = jnp.zeros((8, LANES), F32)

    def gather(v, cx, cy, x_at, x_load, y_slot_of, y_load):
        v = turn(v, 16 * cx + cy)
        if cx:
            a, base = x_at
            if cx > 0:
                v = jnp.where(lane < 16, turn(x_load(a), cy - base), v)
            else:
                v = jnp.where(lane >= 112, turn(x_load(a), 112 - base + cy), v)
        if cy > 0:
            v = jnp.where(slot == 0, turn(y_load(0), -y_slot_of), v)
        elif cy < 0:
            v = jnp.where(slot == 15, turn(y_load(1), 15 - y_slot_of), v)
        return v

    if first:
        def walls(k, carry):
            at = pl.ds(pl.multiple_of(8 * k + 8, 8), 8)
            flag = s_in[at, :]
            for cx in (-1, 0, 1):
                for cy in (-1, 0, 1):
                    wall_ref[(cx + 1) * 3 + cy + 1, at, :] = gather(
                        flag, cx, cy, x_flag_place(cx), lambda a: xs[a, at, :],
                        y_flag_slot(cx), lambda a: ys[a, at, :])
            return carry

        lax.fori_loop(0, TILES, walls, 0, unroll=6)

    def gather_tile(t, buf):
        here = pl.ds(pl.multiple_of(8 * t, 8), 8)
        for i in range(27):
            cx, cy, cz = VELS[i]
            at = here if cz == 0 else pl.ds(8 * t - cz, 8)
            v = star_in[i, at, :]
            if i != 13:
                v = gather(v, cx, cy, x_place(cx, cy, cz), lambda a: xs[a, at, :],
                           y_slot(cx, cz), lambda a: ys[a, at, :])
                wall = wall_ref[(cx + 1) * 3 + cy + 1, at, :]
                v = jnp.where(wall > 0.5, star_in[26 - i, here, :], v)
            buf[i] = v

    def collide_tile(t, buf):
        f = [buf[i] for i in range(27)]
        mom = moments(f)
        if last:
            inv = 1.0 / mom[0]
            macro = mom[0], mom[1] * inv, mom[2] * inv, mom[3] * inv
        else:
            star, macro = collide(f, mom)
            here = pl.ds(pl.multiple_of(8 * t, 8), 8)
            for i in range(27):
                star_out[i, here, :] = star[i]
        row = pl.ds(pl.multiple_of(8 * t - 8, 8), 8)
        for a, v in enumerate(macro):
            mom_out[a, row, :] = v

    even, odd = refs[2:4]

    def pack_at(m):
        if not last:
            pack_pair(m, star_out, None, xp_out, yp_out, ym_out)

    def body(m, carry):
        collide_tile(2 * m + 1, even)
        gather_tile(2 * m + 2, odd)
        pack_at(jnp.maximum(m - 1, 0))
        collide_tile(2 * m + 2, odd)
        gather_tile(jnp.minimum(2 * m + 3, TILES), even)
        return carry

    gather_tile(1, even)
    lax.fori_loop(0, TILES // 2, body, 0)
    pack_at(TILES // 2 - 1)
    if not last:
        xc_out[...] = corners(yp_out[...].astype(F32), ym_out[...].astype(F32)).astype(xc_out.dtype)


def prepare_kernel(capacity, owner_row, owner_col, cell, placing_out, lane_out, row_out):
    slots = owner_row.shape[1]
    q = lax.broadcasted_iota(jnp.int32, (slots, slots), 0)
    p = lax.broadcasted_iota(jnp.int32, (slots, slots), 1)
    same = (owner_row[...] == owner_col[...]) & (q < p)
    rank = jnp.sum(same.astype(F32), axis=0, keepdims=True).astype(jnp.int32)
    column = owner_row[...] * capacity + rank
    rows = placing_out.shape[0]
    placing_out[...] = (lax.broadcasted_iota(jnp.int32, (rows, slots), 0) == column).astype(F32).astype(jnp.bfloat16)
    k = lax.broadcasted_iota(jnp.int32, (LANES, slots), 0)
    lane_out[...] = (k == cell[...] // 128).astype(F32).astype(jnp.bfloat16)
    row_out[...] = (k == cell[...] % 128).astype(F32)


def split3(v):
    hi = v.astype(jnp.bfloat16)
    left = v - hi.astype(F32)
    mid = left.astype(jnp.bfloat16)
    low = (left - mid.astype(F32)).astype(jnp.bfloat16)
    return hi, mid, low


def sample_rows(upper, mom, lane_hot, row_hot, area, placing):
    fields = []
    hot = row_hot[...]
    lanes = lane_hot[...]
    for a in range(4):
        picked = None
        for part in split3(mom[a, 8 : 8 + 128, :]):
            term = jnp.dot(part, lanes, preferred_element_type=F32)
            picked = term if picked is None else picked + term
        fields.append(jnp.sum(picked * hot, axis=0, keepdims=True))
    rho, u = fields[0], fields[1:]
    pressure = (rho - 1.0) / 3.0
    normal = [area[j : j + 1, :] for j in range(3)]
    flow = u[0] * normal[0] + u[1] * normal[1] + u[2] * normal[2]
    rows = [rho * flow] + [pressure * normal[j] + rho * u[j] * flow for j in range(3)]
    blank = [jnp.zeros_like(rho)] * 4
    stacked = jnp.concatenate(blank + rows if upper else rows + blank, axis=0).astype(jnp.bfloat16)
    return lax.dot_general(stacked, placing[...], (((1,), (1,)), ((), ())), preferred_element_type=F32)


def sample_kernel(upper, *refs):
    refs[-1][...] = sample_rows(upper, *refs[:-1])


def scatter_kernel(groups, capacity, mom, lane_hot, row_hot, area, placing, part0, part1, part2, out):
    last = sample_rows(1, mom, lane_hot, row_hot, area, placing)
    pairs = [part0[...] + part1[...], part2[...] + last]
    lane = lane_iota()
    for g in range(groups):
        start = g * capacity
        tile = slice(start // LANES * LANES, start // LANES * LANES + LANES)
        low = turn(pairs[0][:, tile], -start)
        high = turn(pairs[1][:, tile], 64 - start)
        value = jnp.where(lane < 64, low, high)
        out[g] = value


def fetch_kernel(weights_hbm, unused, out, sem):
    copy = pltpu.make_async_copy(weights_hbm.at[pl.ds(0, out.shape[0])], out, sem.at[0])
    copy.start()
    copy.wait()


def window_kernel(solid_hbm, mom, unused, density_out, velocity_out, solid, sem):
    copy = pltpu.make_async_copy(solid_hbm, solid, sem.at[0])
    copy.start()
    copy.wait()
    wall = solid[...] != 0
    density_out[...] = jnp.where(wall, 1.0, mom[0, 8:136, :].T)
    for a in range(3):
        velocity_out[a] = jnp.where(wall, 0.0, mom[a + 1, 8:136, :].T)


def observe_kernel(groups, capacity, ptile, weights_hbm, near, offset, rec, out, rest, sem):
    ahead = near.shape[0]
    copy = pltpu.make_async_copy(weights_hbm.at[pl.ds(ahead, 4 - ahead)], rest, sem.at[0])
    copy.start()
    obs = rest.shape[2]
    part = obs // 2
    tiles = offset.shape[0]
    rows = groups * capacity
    halves = []
    lane = lane_iota()
    per = LANES // capacity
    for half in range(2):
        pieces = []
        for start in range(0, groups, per):
            acc = jnp.zeros((8, LANES), F32)
            for g in range(start, start + per):
                moved = turn(rec[g], (g - start) * capacity - 64 * half)
                acc = jnp.where(lane // capacity == g - start, moved, acc)
            pieces.append(acc)
        halves.append(jnp.concatenate(pieces, axis=1))
    keep = lax.broadcasted_iota(jnp.int32, (tiles, rows), 1) // ptile == lax.broadcasted_iota(jnp.int32, (tiles, rows), 0)
    lefts = []
    for k in range(4):
        left = [
            jnp.where(keep, jnp.broadcast_to(halves[s // 2][4 * (s % 2) + k : 4 * (s % 2) + k + 1, :], (tiles, rows)), 0.0)
            for s in range(STEPS)
        ]
        lefts.append(jnp.concatenate(left, axis=0).astype(jnp.bfloat16))
    devices = out.shape[0]
    count = obs // devices
    obs_tile = obs // offset.shape[1]
    for h in range(2):
        acc = None
        for k in range(4):
            if k == ahead and h == 0:
                copy.wait()
            cols = slice(h * part, (h + 1) * part)
            right = near[k, :, cols] if k < ahead else rest[k - ahead, :, cols]
            term = jnp.dot(lefts[k], right, preferred_element_type=F32)
            acc = term if acc is None else acc + term
        peak = jnp.max(jnp.max(jnp.abs(acc), axis=1, keepdims=True), axis=0, keepdims=True)
        power = jnp.broadcast_to(jnp.ceil(jnp.log2(jnp.maximum(peak, 1e-30))), (tiles, LANES))
        down = jnp.exp2(TOP - power)
        for d in range(h * devices // 2, (h + 1) * devices // 2):
            start = d * count
            here = start - h * part
            piece = jnp.zeros((tiles, LANES), F32)
            for s in range(STEPS):
                block = acc[tiles * s : tiles * (s + 1), here // LANES * LANES : here // LANES * LANES + LANES]
                moved = turn(block, s * count - start % LANES)
                piece = jnp.where(lane // count == s, moved, piece)
            out[d, 0:tiles, :] = piece * down
            o = start // obs_tile
            out[d, tiles : 2 * tiles, :] = jnp.where(lane < 64, jnp.broadcast_to(offset[:, o : o + 1], (tiles, LANES)), power)


def signal_kernel(got, out):
    devices, twice = got.shape[0], got.shape[1]
    tiles = twice // 2
    count = out.shape[0]
    shape = (devices * tiles, LANES)
    notes = got[:, tiles:twice, :].reshape(shape)
    start = jnp.broadcast_to(notes[:, 0:1], shape)
    values = got[:, 0:tiles, :].reshape(shape) * jnp.exp2(jnp.broadcast_to(notes[:, 64:65], shape) - TOP)
    bins = lax.broadcasted_iota(jnp.int32, (devices * tiles, NB), 1).astype(F32)
    hot = (start == bins).astype(F32).astype(jnp.bfloat16)
    acc = None
    for part in split3(values):
        term = lax.dot_general(part, hot, (((0,), (0,)), ((), ())), preferred_element_type=F32)
        acc = term if acc is None else acc + term
    total = None
    for s in range(STEPS):
        moved = turn(acc[s * count : (s + 1) * count, :], s)
        total = moved if total is None else total + moved
    out[...] = total


def call(kernel, outs, *args, scratch=(), flops=1000000, limit=24, far=()):
    args = [pltpu.with_memory_space_constraint(a, pltpu.HBM) if k in far else a for k, a in enumerate(args)]
    return pl.pallas_call(
        kernel,
        out_shape=outs,
        in_specs=[pl.BlockSpec(memory_space=pltpu.HBM if k in far else pltpu.VMEM) for k in range(len(args))],
        out_specs=jax.tree.map(lambda _: pl.BlockSpec(memory_space=pltpu.VMEM), outs),
        scratch_shapes=list(scratch),
        compiler_params=pltpu.CompilerParams(vmem_limit_bytes=limit << 20),
        cost_estimate=pl.CostEstimate(
            flops=flops, transcendentals=0,
            bytes_accessed=sum(a.size * a.dtype.itemsize for a in args)),
    )(*args)


def ring(axis, shift):
    count = lax.axis_size(axis)
    return [(i, (i + shift) % count) for i in range(count)]


def shift(value, axis, by):
    return lax.ppermute(value, axis, ring(axis, by))


def exchange(xp, yp, ym, xc):
    if lax.axis_size("gx") == 2:
        low = high = shift(xc, "gx", 1)
        xh = shift(xp, "gx", 1)
    else:
        low = shift(xc, "gx", 1)
        high = shift(xc, "gx", -1)
        up = shift(jnp.stack([xp[0], xp[2]]), "gx", 1)
        down = shift(jnp.stack([xp[1], xp[2]]), "gx", -1)
        xh = jnp.stack([up[0], down[0], jnp.where(jnp.arange(LANES) < 64, up[1], down[1])])
    face = jax.ShapeDtypeStruct((HALO_ROWS, LANES), HALO_TYPE)
    yp, ym = call(patch_kernel, (face, face), low, high, yp, ym)
    return xh, shift(yp, "gy", 1), shift(ym, "gy", -1)


def shards(perturb, density, velocity, excitation, solid_flag, panel_cell, panel_owner, panel_area, weights, bin_offset):
    bx, by, bz = density.shape
    assert bx * by == LANES and bz == LANES and by == 16
    flat = (LANES, LANES)
    solid = solid_flag.reshape(flat)
    block = jax.ShapeDtypeStruct((27, ROWS, LANES), F32)
    one = jax.ShapeDtypeStruct((ROWS, LANES), F32)
    rim = jax.ShapeDtypeStruct((28 * 4, LANES), HALO_TYPE)
    x_face = jax.ShapeDtypeStruct((3, HALO_ROWS, LANES), HALO_TYPE)
    y_face = jax.ShapeDtypeStruct((HALO_ROWS, LANES), HALO_TYPE)
    x_edge = jax.ShapeDtypeStruct((FOLD, LANES), HALO_TYPE)

    f0, low_rim, high_rim, flags = call(
        initial_kernel, (block, rim, rim, one),
        perturb.reshape((27,) + flat), density.reshape(flat), velocity.reshape((3,) + flat),
        excitation.reshape(flat), solid,
        far=range(5),
        scratch=(pltpu.VMEM((27,) + flat, F32), pltpu.VMEM(flat, F32), pltpu.VMEM((3,) + flat, F32), pltpu.VMEM(flat, F32),
                 pltpu.VMEM(flat, jnp.int32), pltpu.VMEM((112, LANES), F32), pltpu.VMEM((112, LANES), F32), pltpu.SemaphoreType.DMA((9,)), pltpu.SemaphoreType.DMA((4,))))
    below = lax.ppermute(high_rim, "gz", ring("gz", 1))
    above = lax.ppermute(low_rim, "gz", ring("gz", -1))

    group_count = lax.axis_size(("gx", "gy"))
    slots = panel_owner.shape[0]
    row_count = 2 * slots
    capacity = row_count // group_count
    placing, lane_hot, row_hot = call(
        functools.partial(prepare_kernel, capacity),
        (jax.ShapeDtypeStruct((row_count, slots), jnp.bfloat16),
         jax.ShapeDtypeStruct((LANES, slots), jnp.bfloat16),
         jax.ShapeDtypeStruct((LANES, slots), F32)),
        panel_owner.reshape(1, slots), panel_owner.reshape(slots, 1), panel_cell.reshape(1, slots))

    star, walls, xp, yp, ym, xc = call(
        first_kernel, (block, one, x_face, y_face, y_face, x_edge), f0, flags, below, above, placing,
        scratch=(pltpu.VMEM((28, 16, LANES), F32), pltpu.VMEM((112, LANES), F32), pltpu.VMEM((112, LANES), F32)))

    mom_shape = jax.ShapeDtypeStruct((4, HALO_ROWS, LANES), F32)
    routed = []
    for s in range(STEPS):
        first, last = s == 0, s == STEPS - 1
        xh, yph, ymh = exchange(xp, yp, ym, xc)
        outs = [mom_shape]
        if not last:
            outs += [block, x_face, y_face, y_face, x_edge]
        if first:
            outs += [jax.ShapeDtypeStruct((9, ROWS, LANES), F32)]
        scratch = [pltpu.VMEM((3, ROWS, LANES), F32), pltpu.VMEM((2, ROWS, LANES), F32)]
        scratch += [pltpu.VMEM((27, 8, LANES), F32)] * 2
        res = call(functools.partial(step_kernel, first, last), tuple(outs), star, walls, xh, yph, ymh,
                   routed[-1] if routed else placing, scratch=scratch)
        mom = res[0]
        if not last:
            star, xp, yp, ym, xc = res[1:6]
        if first:
            walls = res[6]
        if not last:
            routed.append(call(functools.partial(sample_kernel, s % 2), jax.ShapeDtypeStruct((8, row_count), F32),
                               mom, lane_hot, row_hot, panel_area, placing))

    send = functools.partial(scatter_kernel, group_count, capacity)
    samples = (mom, lane_hot, row_hot, panel_area, placing, *routed)

    def fetch(count, after):
        return call(fetch_kernel,
                    jax.ShapeDtypeStruct((count,) + weights.shape[1:], weights.dtype), weights, after, far=(0,),
                    scratch=(pltpu.SemaphoreType.DMA((1,)),))

    sent = call(send, jax.ShapeDtypeStruct((group_count, 8, LANES), F32), *samples)
    received = lax.all_to_all(sent, ("gx", "gy"), split_axis=0, concat_axis=0, tiled=True)
    near = fetch(3, sent)

    tiles, obs_tiles = bin_offset.shape
    devices = lax.axis_size(("gx", "gy", "gz"))
    obs = weights.shape[2]
    count = obs // devices
    assert obs // obs_tiles % count == 0 and tiles % 8 == 0 and STEPS * count <= LANES and capacity <= 64
    out_shape = (devices, 2 * tiles, LANES)
    observed = pl.pallas_call(
        functools.partial(observe_kernel, group_count, capacity, row_count // tiles),
        out_shape=jax.ShapeDtypeStruct(out_shape, F32),
        in_specs=[pl.BlockSpec(memory_space=pltpu.HBM)] + [pl.BlockSpec(memory_space=pltpu.VMEM)] * 3,
        out_specs=pl.BlockSpec(memory_space=pltpu.VMEM),
        scratch_shapes=[pltpu.VMEM((4 - near.shape[0],) + weights.shape[1:], weights.dtype),
                        pltpu.SemaphoreType.DMA((1,))],
        compiler_params=pltpu.CompilerParams(vmem_limit_bytes=24 << 20),
    )(pltpu.with_memory_space_constraint(weights, pltpu.HBM), near, bin_offset.astype(F32), received)
    final_density, final_velocity = call(
        window_kernel,
        (jax.ShapeDtypeStruct(flat, F32), jax.ShapeDtypeStruct((3,) + flat, F32)),
        solid, mom, sent, far=(0,), scratch=(pltpu.VMEM(flat, jnp.int32), pltpu.SemaphoreType.DMA((1,))))
    got = lax.all_to_all(observed.astype(jnp.float16), ("gx", "gy", "gz"), split_axis=0, concat_axis=0, tiled=True)
    signal = call(signal_kernel, jax.ShapeDtypeStruct((count, NB), F32), got.astype(F32))
    return final_density.reshape(density.shape), final_velocity.reshape(velocity.shape), signal


def solution(mesh):
    cells = P("gx", "gy", "gz")
    vectors = P(None, "gx", "gy", "gz")
    every = ("gx", "gy", "gz")
    placed = (vectors, cells, vectors, cells, cells, P(every), P(every), P(None, every), P(None, every, None), P(every, None))
    return jax.shard_map(
        shards, mesh=mesh, in_specs=placed, out_specs=(cells, vectors, P(every, None)), check_vma=False)
```
